32 devices in a mesh: tm: 4 (over y, core), lat: 4 (over z), lon: 2 (over x).
Axes of the slice: x: 2, y: 2, z: 4, core: 2. Of those that a mesh axis runs over, the one named last changes fastest.
Arguments:
- state: bfloat16 [4, 4, 137, 32, 512], P('tm', None, None, 'lat', 'lon'), may hold values from -6 to 6
- band_counts: int32 [4, 4], P('tm', 'lat'), may hold values from 2 to 6
- dep_blocks: int32 [4, 32, 4, 6], P('tm', 'lat', 'lon'), may hold values from 0 to 3, as said below
- lon_entry: int32 [4, 32, 512], P('tm', 'lat', 'lon'), may hold values from 0 to 5
- lon_offset: int32 [4, 32, 512], P('tm', 'lat', 'lon'), may hold values from 1 to 125
- lon_frac: float32 [4, 32, 512], P('tm', 'lat', 'lon'), may hold values from 0 to 1
- lat_offset: int32 [4, 32, 512], P('tm', 'lat', 'lon'), may hold values from -1 to 0
- lat_frac: float32 [4, 32, 512], P('tm', 'lat', 'lon'), may hold values from 0 to 1
Outputs:
- misfit: bfloat16 [4, 4, 137, 32, 512], P('tm', None, None, 'lat', 'lon')
The draws below stay inside these ranges and needn't reach their ends.
Inputs may be any that keep to these rules, and one draw needn't show every extreme that they name: `dep_blocks`: the list of a destination block names each of the 6 blocks of its latitude row that lie from 3 blocks west of the first block of the destination's tile to 1 block east of the tile's last block (block numbers taken modulo 4) exactly once, in an order drawn for each block.
All inputs are finite; a program needn't handle non-finite values.
Results may differ from the reference program's by a relative error of at most 0.0046.
Values may be sent and summed in bfloat16 or wider, within the bound.
A program may use at most 64 MiB of HBM per device.

```python
import jax
import jax.numpy as jnp
from jax import lax

VARS = 4
LEV = 137
BLK = 128
NB = 2
RL = 8
KMAX = 6
WINDOWS = 4
BANDS = 4
NROWS = 32
CYCLE = 4
COLS = 512


def draw_dep_blocks(key, part):
    keyed = jax.random.fold_in(jax.random.fold_in(key, 202), part)
    scores = jax.random.randint(jax.random.fold_in(keyed, 21), (WINDOWS, NROWS, CYCLE, KMAX), 0, 2 ** 20, dtype=jnp.int32)
    scores = scores * KMAX + jnp.arange(KMAX, dtype=jnp.int32)
    ordering = jnp.argsort(scores, axis=-1, stable=True).astype(jnp.int32)
    block_index = jnp.arange(CYCLE, dtype=jnp.int32)
    tile_start = block_index // NB * NB
    return ((tile_start[None, None, :, None] - NB - NB // 2 + ordering) % CYCLE).astype(jnp.int32)


def place_ends(entries, key, smallest, top_value):
    place = [jax.random.randint(jax.random.fold_in(key, axis), (), 0, length) for axis, length in enumerate(entries.shape)]
    longest = entries.shape.index(max(entries.shape))
    neighbour = place[:longest] + [(place[longest] + 1) % entries.shape[longest]] + place[longest + 1:]
    return entries.at[tuple(place)].set(smallest).at[tuple(neighbour)].set(top_value)


def block_scale(stream_key, shape, split, least, top_value):
    level, own = 1.0, jax.random.fold_in(stream_key, 6)
    for dim, parts in split:
        heights = jnp.exp(jax.random.uniform(jax.random.fold_in(own, dim), (parts,), jnp.float32, least / len(split), top_value / len(split)))
        level = level * jnp.repeat(heights, shape[dim] // parts).reshape([-1 if axis == dim else 1 for axis in range(len(shape))])
    return level


def gaussian(rng, dims, spread, bound, cuts=(), kind=jnp.bfloat16):
    factor_of = block_scale(rng, dims, cuts, -0.22, 0.18) if cuts else 1.0
    result = jax.random.normal(rng, dims, jnp.float32) * spread * factor_of
    return jnp.minimum(jnp.maximum(result, -bound), bound).astype(kind)


def setup_inputs(seed: int = 0) -> dict:
    splits = jax.random.split(jax.random.key(seed), 9)
    state = gaussian(splits[0], (WINDOWS, VARS, LEV, NROWS, COLS), 1.0, 6.0, ((0, 4), (3, 4), (4, 2)))
    band_counts = place_ends(jax.random.randint(splits[1], (WINDOWS, BANDS), 2, KMAX + 1), jax.random.fold_in(splits[1], 1), 2, KMAX).astype(jnp.int32)
    dep_blocks = draw_dep_blocks(jax.random.fold_in(splits[8], 71), 0)
    lon_entry = place_ends(jax.random.randint(splits[3], (WINDOWS, NROWS, COLS), 0, KMAX), jax.random.fold_in(splits[3], 1), 0, KMAX - 1).astype(jnp.int32)
    lon_offset = place_ends(jax.random.randint(splits[4], (WINDOWS, NROWS, COLS), 1, BLK - 2), jax.random.fold_in(splits[4], 1), 1, (BLK - 2) - 1).astype(jnp.int32)
    lon_frac = jnp.clip(1.0 * jax.random.uniform(splits[5], (WINDOWS, NROWS, COLS), jnp.float32) ** block_scale(splits[5], (WINDOWS, NROWS, COLS), ((0, 4), (1, 4), (2, 2)), -0.2, 0.2), 0.0, 1.0)
    lat_offset = place_ends(jax.random.randint(splits[6], (WINDOWS, NROWS, COLS), -1, 1), jax.random.fold_in(splits[6], 1), -1, 0).astype(jnp.int32)
    lat_frac = jnp.clip(1.0 * jax.random.uniform(splits[7], (WINDOWS, NROWS, COLS), jnp.float32) ** block_scale(splits[7], (WINDOWS, NROWS, COLS), ((0, 4), (1, 4), (2, 2)), -0.2, 0.2), 0.0, 1.0)
    return {"state": state, "band_counts": band_counts, "dep_blocks": dep_blocks, "lon_entry": lon_entry, "lon_offset": lon_offset, "lon_frac": lon_frac, "lat_offset": lat_offset, "lat_frac": lat_frac}


def cubic_weights(fraction):
    return jnp.stack([
        -fraction * (fraction - 1.0) * (fraction - 2.0) / 6.0,
        (fraction + 1.0) * (fraction - 1.0) * (fraction - 2.0) / 2.0,
        -(fraction + 1.0) * fraction * (fraction - 2.0) / 2.0,
        (fraction + 1.0) * fraction * (fraction - 1.0) / 6.0,
    ])


def reference(state, band_counts, dep_blocks, lon_entry, lon_offset, lon_frac, lat_offset, lat_frac):
    depth_rows = VARS * LEV
    windows = state.reshape(WINDOWS, depth_rows, NROWS, COLS)
    band_of_row = jnp.arange(NROWS, dtype=jnp.int32) // RL
    block_of_col = jnp.arange(COLS, dtype=jnp.int32) // BLK
    stencil_nodes = jnp.arange(4, dtype=jnp.int32)

    def one_window(previous, window):
        fields, counts, departure_lists, entry_rows, offset_rows, fraction_rows, lat_shift, lat_fraction = window
        by_row = jnp.swapaxes(fields, 0, 1)

        def one_row(row_data):
            source_row, list_row, entry_row, offset_row, fraction_row, band_index = row_data
            entry_slot = entry_row % counts[band_index]
            chosen = jnp.take_along_axis(list_row[block_of_col], entry_slot[:, None], axis=1)[:, 0]
            positions = (chosen[:, None] * BLK + offset_row[:, None] - 1 + stencil_nodes[None, :]).astype(jnp.int32)
            rounded = lax.optimization_barrier(cubic_weights(fraction_row).astype(jnp.bfloat16))
            weights = rounded.astype(jnp.float32)
            picked = source_row[:, positions].astype(jnp.float32)
            return jnp.sum(picked * weights.T[None, :, :], axis=2).astype(jnp.bfloat16)

        advected = lax.map(one_row, (by_row, departure_lists, entry_rows, offset_rows, fraction_rows, band_of_row))
        padded = jnp.pad(advected, ((2, 2), (0, 0), (0, 0)))
        lat_weights = cubic_weights(lat_fraction)
        end_sum = jnp.zeros((NROWS, depth_rows, COLS), jnp.float32)
        for shift_rows in range(-2, 3):
            coefficient = jnp.zeros((NROWS, COLS), jnp.float32)
            for node_index in range(4):
                coefficient = coefficient + jnp.where(lat_shift + node_index - 1 == shift_rows, lat_weights[node_index], 0.0)
            end_sum = end_sum + coefficient[:, None, :] * padded[2 + shift_rows:2 + shift_rows + NROWS].astype(jnp.float32)
        end_state = end_sum.astype(jnp.bfloat16)
        misfit_rows = (by_row.astype(jnp.float32) - previous.astype(jnp.float32)).astype(jnp.bfloat16)
        return end_state, misfit_rows

    start = jnp.zeros((NROWS, depth_rows, COLS), jnp.bfloat16)
    _, misfits = lax.scan(one_window, start, (windows, band_counts, dep_blocks, lon_entry, lon_offset, lon_frac, lat_offset, lat_frac))
    return jnp.swapaxes(misfits, 1, 2).reshape(WINDOWS, VARS, LEV, NROWS, COLS)
```

```python
import functools

import jax
import jax.numpy as jnp
from jax import lax
from jax.experimental import pallas as pl
from jax.experimental.pallas import tpu as pltpu
from jax.sharding import PartitionSpec as P

BLK = 128
CHUNK = 56
TAIL = 16
MESH = pl.DeviceIdType.MESH


def cubic_weights(fraction):
    return [
        -fraction * (fraction - 1.0) * (fraction - 2.0) / 6.0,
        (fraction + 1.0) * (fraction - 1.0) * (fraction - 2.0) / 2.0,
        -(fraction + 1.0) * fraction * (fraction - 2.0) / 2.0,
        (fraction + 1.0) * fraction * (fraction - 1.0) / 6.0,
    ]


def source_plan(blocks, devices):
    spread = blocks + blocks // 2
    count = min(3 * blocks, blocks * devices)
    slots, pieces, at = [None] * count, [], blocks
    for q in range(count):
        offset, block = divmod(q - spread, blocks)
        if offset % devices == 0:
            slots[q] = block
            continue
        if pieces and pieces[-1][0] == offset and pieces[-1][1] + pieces[-1][2] == block:
            pieces[-1][2] += 1
        else:
            pieces.append([offset, block, 1, at])
        slots[q] = at
        at += 1
    return slots, [tuple(piece) for piece in pieces], at


def span_plan(depth):
    big = max((depth - 1) // CHUNK, 0)
    left = depth - big * CHUNK
    small = -(-left // TAIL)
    return big, small, left - (small - 1) * TAIL


def work_plan(n_tm, big):
    helping = n_tm >= 4
    helped = n_tm - 3
    half = (big + 1) // 2
    pairs = []
    for owner in range(n_tm - 1):
        low = half if helping and owner == helped else 0
        pairs.append((owner, owner + 1, low, big, True, owner % 2 == 0))
    if helping:
        pairs.append((helped, 0, 0, half, False, True))
    return helping, helped, half, pairs


def meeting_plan(n_tm, n_lon, pairs, pieces, helping, helped):
    met = [set() for _ in range(n_tm)]

    def meet(a, b, shift):
        if a != b or shift % n_lon:
            met[a].add((b, shift % n_lon))
            met[b].add((a, -shift % n_lon))

    for owner, worker, _, _, _, direct in pairs:
        meet(owner, worker, 0)
        for piece in pieces:
            meet(owner if direct else worker, worker, -piece[0])
    if helping:
        meet(0, helped + 1, 0)
    return [sorted(entry) for entry in met]


def kernel(plan, spans, depth, sizes, state, counts, lists, *rest_refs):
    slots, pieces, n_src = plan
    big, small, rest = spans
    arrays, result, scratch = rest_refs[:5], rest_refs[5], rest_refs[6:]
    n_tm, n_lat, n_lon = sizes
    n_pieces = len(pieces)
    own, remotes = scratch[0], scratch[1 : 1 + n_pieces]
    (
        mine, prev, m_sem, counts_s, lists_s, *arrays_v, flat, params, given, matrix, adv, f_end, ends, own_send,
        own_recv, x_send, f_send, x_recv, h_send, h_recv, t_send, t_recv, p_send, p_recv, a_sem,
    ) = scratch[1 + n_pieces :]
    rows, cols = state.shape[1:]
    tm, lat, lon = lax.axis_index("tm"), lax.axis_index("lat"), lax.axis_index("lon")
    helping, helped, half, pairs = work_plan(n_tm, big)
    chunks = big + small

    is_helper = tm == 0
    first, last = jnp.int32(0), jnp.int32(0)
    for _, worker, low, high, _, _ in pairs:
        first = jnp.where(tm == worker, low, first)
        last = jnp.where(tm == worker, high, last)
    tailed = tm > 0

    aux = [
        pltpu.make_async_copy(source, place, a_sem.at[i])
        for i, (source, place) in enumerate(
            [(counts, counts_s), (lists, lists_s)]
            + [(array.at[0], place) for array, place in zip(arrays, arrays_v)]
        )
    ]
    to_mine = pltpu.make_async_copy(state, mine, m_sem)
    to_result = pltpu.make_async_copy(state, result, m_sem)
    owning = tm < n_tm - 1

    barrier = pltpu.get_barrier_semaphore()
    greeted = jnp.int32(0)

    def greet(condition, devices):
        @pl.when(condition)
        def _():
            for device in devices:
                pl.semaphore_signal(barrier, inc=1, device_id=device, device_id_type=MESH)

        return jnp.where(condition, len(devices), 0)

    for t, entry in enumerate(meeting_plan(n_tm, n_lon, pairs, pieces, helping, helped)):
        greeted += greet(
            tm == t, [{"tm": jnp.int32(b), "lon": lax.rem(lon + shift, n_lon)} for b, shift in entry]
        )
    greeted += greet(lat > 0, [{"lat": lat - 1}]) + greet(lat < n_lat - 1, [{"lat": lat + 1}])

    @pl.when(owning)
    def _():
        for copy in aux:
            copy.start()

    pl.semaphore_wait(barrier, greeted)

    def span(k):
        if isinstance(k, int) and k >= big:
            s = k - big
            return (depth - rest, rest) if s == small - 1 else (big * CHUNK + s * TAIL, TAIL)
        return k * CHUNK, CHUNK

    def own_copy(worker, k):
        part = pl.ds(*span(k))
        return pltpu.make_async_remote_copy(
            src_ref=state.at[part], dst_ref=own.at[part], send_sem=own_send.at[k], recv_sem=own_recv.at[k],
            device_id={"tm": jnp.int32(worker)}, device_id_type=MESH,
        )

    def x_copies(worker, k, direct):
        part = pl.ds(*span(k))
        source, sems = (state, x_send) if direct else (own, f_send)
        copies = []
        for i, (offset, block, number, _) in enumerate(pieces):
            copies.append(
                pltpu.make_async_remote_copy(
                    src_ref=source.at[part, :, pl.ds(block * BLK, number * BLK)],
                    dst_ref=remotes[i].at[part],
                    send_sem=sems.at[i, k], recv_sem=x_recv.at[i, k],
                    device_id={"tm": jnp.int32(worker), "lon": lax.rem(lon - offset + 2 * n_lon, n_lon)},
                    device_id_type=MESH,
                )
            )
        return copies

    def prm_copy(worker, slot):
        return pltpu.make_async_remote_copy(
            src_ref=params, dst_ref=given, send_sem=p_send.at[slot], recv_sem=p_recv,
            device_id={"tm": jnp.int32(worker)}, device_id_type=MESH,
        )

    def halo_up(k, size):
        return pltpu.make_async_remote_copy(
            src_ref=adv.at[k, pl.ds(rows, 2), pl.ds(0, size)], dst_ref=adv.at[k, pl.ds(0, 2), pl.ds(0, size)],
            send_sem=h_send.at[0, k], recv_sem=h_recv.at[0, k],
            device_id={"lat": lat + 1}, device_id_type=MESH,
        )

    def halo_down(k, size):
        return pltpu.make_async_remote_copy(
            src_ref=adv.at[k, pl.ds(2, 2), pl.ds(0, size)],
            dst_ref=adv.at[k, pl.ds(rows + 2, 2), pl.ds(0, size)],
            send_sem=h_send.at[1, k], recv_sem=h_recv.at[1, k],
            device_id={"lat": lat - 1}, device_id_type=MESH,
        )

    def end_copy(k):
        return pltpu.make_async_remote_copy(
            src_ref=ends.at[k], dst_ref=prev.at[pl.ds(k * CHUNK, CHUNK)], send_sem=t_send.at[k], recv_sem=t_recv.at[k],
            device_id={"tm": jnp.int32(helped + 1)}, device_id_type=MESH,
        )

    def loop(low, high, act):
        lax.fori_loop(low, high, lambda c, _: (act(c), 0)[1], 0)

    def over(low, high, tail, act):
        loop(low, high, act)
        if tail:
            for k in range(big, chunks):
                act(k)

    def start_all(copies):
        for copy in copies:
            copy.start()

    for owner, worker, low, high, tail, direct in pairs:

        @pl.when(tm == owner)
        def _():
            if direct:
                start_all(x_copies(worker, low, True))
                loop(low, low + 2, lambda k: own_copy(worker, k).start())
                over(low + 1, high, tail, lambda k: start_all(x_copies(worker, k, True)))
                over(low + 2, high, tail, lambda k: own_copy(worker, k).start())
            else:
                over(low, high, tail, lambda k: own_copy(worker, k).start())

    pl.when(tm > 0)(to_mine.start)
    pl.when(tm == 0)(to_result.start)

    @pl.when(lat == 0)
    def _():
        adv[:, 0:2] = jnp.zeros((chunks, 2, CHUNK, cols), adv.dtype)

    @pl.when(lat == n_lat - 1)
    def _():
        adv[:, rows + 2 : rows + 4] = jnp.zeros((chunks, 2, CHUNK, cols), adv.dtype)

    def prepare():
        for copy in aux:
            copy.wait()
        entry, offset, lon_fraction, lat_shift, lat_fraction = [v[...] for v in arrays_v]
        per_list = lists.shape[1]
        for _ in range((per_list - 1) // 2):
            entry = jnp.where(entry >= counts_s[0, 0], entry - counts_s[0, 0], entry)
        blocks = cols // BLK
        total = blocks * n_lon
        for r in range(rows):
            for g in range(blocks):
                wanted = entry[r : r + 1, g * BLK : (g + 1) * BLK]
                chosen = jnp.zeros((1, BLK), jnp.int32)
                for k in range(per_list):
                    q = lists_s[0, k, g, r] - lon * blocks + blocks + blocks // 2 + total
                    q = lax.rem(q, total)
                    slot = jnp.int32(slots[0])
                    for i in range(1, len(slots)):
                        slot = jnp.where(q == i, slots[i], slot)
                    chosen = jnp.where(wanted == k, slot, chosen)
                params[1, r : r + 1, g * BLK : (g + 1) * BLK] = chosen.astype(jnp.float32)
        params[0] = offset.astype(jnp.float32)
        for node, weight in enumerate(cubic_weights(lon_fraction)):
            params[2 + node] = weight.astype(jnp.bfloat16).astype(jnp.float32)
        lat_weights = cubic_weights(lat_fraction)
        for shift in range(-2, 3):
            coefficient = jnp.zeros((rows, cols), jnp.float32)
            for node in range(4):
                coefficient = coefficient + jnp.where(
                    lat_shift + node - 1 == shift, lat_weights[node], 0.0
                )
            params[8 + shift] = coefficient

    def build(r):
        offset, slot = given[0, pl.ds(r, 1), :], given[1, pl.ds(r, 1), :]
        gap = lax.broadcasted_iota(jnp.int32, (BLK, cols), 0).astype(jnp.float32) - offset
        value = jnp.zeros((BLK, cols), jnp.float32)
        for node in range(4):
            weight = given[2 + node, pl.ds(r, 1), :]
            value = jnp.where(gap == node - 1.0, weight, value)
        for q in range(n_src):
            matrix[r, q * BLK : (q + 1) * BLK, :] = jnp.where(slot == q, value, 0.0).astype(
                jnp.bfloat16
            )

    def advect(k, begin, size):
        at = 0
        for buffer in (own, *remotes):
            for b in range(buffer.shape[2] // BLK):
                part = buffer[pl.ds(begin, size), :, b * BLK : (b + 1) * BLK].astype(jnp.float32)
                flat[at, 0 : size * rows] = part.reshape(size * rows, BLK)
                at += 1
        for r in [0, 1, rows - 2, rows - 1] + list(range(2, rows - 2)):
            parts = [
                flat[q, pl.ds(r, size, stride=rows), :].astype(jnp.bfloat16)
                for q in range(n_src)
            ]
            total = jnp.dot(
                jnp.concatenate(parts, axis=1), matrix[r], preferred_element_type=jnp.float32
            )
            adv[k, r + 2, 0:size] = total.astype(adv.dtype)
            if r == 2:

                @pl.when(lat < n_lat - 1)
                def _():
                    halo_up(k, size).start()

                @pl.when(lat > 0)
                def _():
                    halo_down(k, size).start()

    def finish(k, begin, size):
        def interpolate(r):
            total = None
            for shift in range(5):
                term = given[6 + shift, r : r + 1, :] * adv[k, r + shift, 0:size].astype(jnp.float32)
                total = term if total is None else total + term
            for b in range(cols // BLK):
                f_end[b, pl.ds(r, size, stride=rows), :] = total[:, b * BLK : (b + 1) * BLK]

        for r in range(2, rows - 2):
            interpolate(r)

        @pl.when(lat > 0)
        def _():
            halo_up(k, size).wait_recv()

        @pl.when(lat < n_lat - 1)
        def _():
            halo_down(k, size).wait_recv()

        for r in (0, 1, rows - 2, rows - 1):
            interpolate(r)

        @pl.when(tailed)
        def _():
            for b in range(cols // BLK):
                part = f_end[b, 0 : size * rows].reshape(size, rows, BLK).astype(ends.dtype)
                place = (pl.ds(begin, size), slice(None), slice(b * BLK, (b + 1) * BLK))
                result[place] = (mine[place].astype(jnp.float32) - part.astype(jnp.float32)).astype(result.dtype)

        if helping and size == CHUNK:

            @pl.when(is_helper)
            def _():
                for b in range(cols // BLK):
                    part = f_end[b].reshape(CHUNK, rows, BLK).astype(ends.dtype)
                    ends[k, :, :, b * BLK : (b + 1) * BLK] = part
                end_copy(k).start()

    def collect(k):
        place = pl.ds(k * CHUNK, CHUNK)
        end_copy(k).wait_recv()
        moved = prev[place].astype(jnp.float32)
        result[place] = (mine[place].astype(jnp.float32) - moved).astype(result.dtype)

    def tail_place(s):
        return min(big * CHUNK + s * TAIL, depth - TAIL)

    def advect_tail(s):
        advect(big + s, tail_place(s), TAIL)

    pl.when(owning)(prepare)

    routes = [(owner, worker) for owner, worker, *_ in pairs]
    for slot, (owner, worker) in enumerate(routes):
        pl.when(tm == owner)(prm_copy(worker, slot).start)

    for _, worker, low, high, tail, direct in pairs:
        if not direct:

            @pl.when(tm == worker)
            def _():
                def forward(k):
                    own_copy(0, k).wait_recv()
                    start_all(x_copies(worker, k, False))

                over(low, high, tail, forward)

    forwarders = [worker for _, worker, _, _, _, direct in pairs if not direct]
    direct_own = jnp.bool_(True)
    for worker in forwarders:
        direct_own = jnp.logical_and(direct_own, tm != worker)

    def land(k):
        @pl.when(direct_own)
        def _():
            own_copy(0, k).wait_recv()

        for copy in x_copies(0, k, True):
            copy.wait_recv()

    collector = tm == helped + 1

    @pl.when(jnp.logical_or(tailed, first < last))
    def _():
        prm_copy(0, 0).wait_recv()
        loop(0, rows, build)
        pl.when(tailed)(to_mine.wait)

        def step(c):
            @pl.when(c < last)
            def _():
                land(c)
                advect(c, c * CHUNK, CHUNK)

            @pl.when(jnp.logical_and(c == last, tailed))
            def _():
                land(big)
                advect_tail(0)

            @pl.when(c > first)
            def _():
                finish(c - 1, (c - 1) * CHUNK, CHUNK)

            if helping:

                @pl.when(jnp.logical_and(collector, c - first < half))
                def _():
                    collect(c - first)

        loop(first, last + 1, step)

    if helping:

        @pl.when(collector)
        def _():
            loop(jnp.minimum(last + 1 - first, half), half, collect)

    @pl.when(tailed)
    def _():
        for s in range(1, small + 1):
            if s < small:
                land(big + s)
                advect_tail(s)
            finish(big + s - 1, tail_place(s - 1), TAIL)

    pl.when(tm == 0)(to_result.wait)

    for slot, (owner, worker, low, high, tail, direct) in enumerate(pairs):

        @pl.when(tm == owner)
        def _():
            prm_copy(worker, slot).wait_send()

            def sent(k):
                own_copy(worker, k).wait_send()
                if direct:
                    for copy in x_copies(worker, k, True):
                        copy.wait_send()

            over(low, high, tail, sent)

        @pl.when(tm == worker)
        def _():
            def settle(k):
                size = CHUNK if not isinstance(k, int) or k < big else TAIL
                if not direct:
                    for copy in x_copies(worker, k, False):
                        copy.wait_send()

                @pl.when(lat < n_lat - 1)
                def _():
                    halo_up(k, size).wait_send()

                @pl.when(lat > 0)
                def _():
                    halo_down(k, size).wait_send()

                if worker == 0:
                    end_copy(k).wait_send()

            over(low, high, tail, settle)


def body(sizes, state, band_counts, dep_blocks, lon_entry, lon_offset, lon_frac, lat_offset, lat_frac):
    fields_n, levels, rows, cols = state.shape[1:]
    depth, blocks = fields_n * levels, cols // BLK
    n_tm, n_lat, n_lon = sizes
    plan = source_plan(blocks, n_lon)
    _, pieces, n_src = plan
    spans = span_plan(depth)
    big, small, _ = spans
    chunks = big + small
    helping, _, half, pairs = work_plan(n_tm, big)
    flat = state.reshape(depth, rows, cols)

    lists = jnp.transpose(dep_blocks, (0, 3, 2, 1))
    dma = pltpu.SemaphoreType.DMA
    n_pieces = len(pieces)
    misfit = pl.pallas_call(
        functools.partial(kernel, plan, spans, depth, sizes),
        out_shape=pltpu.VMEM(flat.shape, flat.dtype),
        in_specs=[pl.BlockSpec(memory_space=pltpu.HBM)] * 8,
        out_specs=pl.BlockSpec(memory_space=pltpu.VMEM),
        scratch_shapes=[
            pltpu.VMEM(flat.shape, flat.dtype),
            *[pltpu.VMEM((depth, rows, p[2] * BLK), flat.dtype) for p in pieces],
            pltpu.VMEM(flat.shape, flat.dtype),
            pltpu.VMEM(flat.shape, flat.dtype),
            dma(()),
            pltpu.SMEM(band_counts.shape, jnp.int32),
            pltpu.SMEM(lists.shape, jnp.int32),
            *[
                pltpu.VMEM((rows, cols), kind.dtype)
                for kind in (lon_entry, lon_offset, lon_frac, lat_offset, lat_frac)
            ],
            pltpu.VMEM((n_src, CHUNK * rows, BLK), jnp.float32),
            pltpu.VMEM((11, rows, cols), jnp.float32),
            pltpu.VMEM((11, rows, cols), jnp.float32),
            pltpu.VMEM((rows, n_src * BLK, cols), jnp.bfloat16),
            pltpu.VMEM((chunks, rows + 4, CHUNK, cols), flat.dtype),
            pltpu.VMEM((blocks, CHUNK * rows, BLK), jnp.float32),
            pltpu.VMEM((max(half, 1), CHUNK, rows, cols), flat.dtype),
            dma((chunks,)),
            dma((chunks,)),
            dma((n_pieces, chunks)),
            dma((n_pieces, chunks)),
            dma((n_pieces, chunks)),
            dma((2, chunks)),
            dma((2, chunks)),
            dma((max(half, 1),)),
            dma((max(half, 1),)),
            dma((len(pairs),)),
            dma(()),
            dma((7,)),
        ],
        compiler_params=pltpu.CompilerParams(
            collective_id=0, has_side_effects=True, vmem_limit_bytes=60 * 1024 * 1024
        ),
    )(
        pltpu.with_memory_space_constraint(flat, pltpu.HBM),
        band_counts,
        *[
            pltpu.with_memory_space_constraint(array, pltpu.HBM)
            for array in (lists, lon_entry, lon_offset, lon_frac, lat_offset, lat_frac)
        ],
    )
    return misfit.reshape(state.shape)


def solution(mesh):
    placed = (
        P("tm", None, None, "lat", "lon"),
        P("tm", "lat"),
        P("tm", "lat", "lon", None),
        P("tm", "lat", "lon"),
        P("tm", "lat", "lon"),
        P("tm", "lat", "lon"),
        P("tm", "lat", "lon"),
        P("tm", "lat", "lon"),
    )
    sizes = tuple(mesh.shape[name] for name in ("tm", "lat", "lon"))
    return jax.shard_map(
        functools.partial(body, sizes),
        mesh=mesh,
        in_specs=placed,
        out_specs=P("tm", None, None, "lat", "lon"),
        check_vma=False,
    )
```

```python
import functools

import jax
import jax.numpy as jnp
from jax import lax
from jax.experimental import pallas as pl
from jax.experimental.pallas import tpu as pltpu
from jax.sharding import PartitionSpec as P

BLK = 128
CHUNK = 44
TAIL = 152
EDGE = 2
SHARE = 0.48
MESH = pl.DeviceIdType.MESH


def cubic_weights(fraction):
    return [
        -fraction * (fraction - 1.0) * (fraction - 2.0) / 6.0,
        (fraction + 1.0) * (fraction - 1.0) * (fraction - 2.0) / 2.0,
        -(fraction + 1.0) * fraction * (fraction - 2.0) / 2.0,
        (fraction + 1.0) * fraction * (fraction - 1.0) / 6.0,
    ]


def source_plan(blocks, devices):
    spread = blocks + blocks // 2
    count = min(3 * blocks, blocks * devices)
    slots, pieces, at = [None] * count, [], blocks
    for q in range(count):
        offset, block = divmod(q - spread, blocks)
        if offset % devices == 0:
            slots[q] = block
            continue
        if pieces and pieces[-1][0] == offset and pieces[-1][1] + pieces[-1][2] == block:
            pieces[-1][2] += 1
        else:
            pieces.append([offset, block, 1, at])
        slots[q] = at
        at += 1
    return slots, [tuple(piece) for piece in pieces], at


def span_plan(depth):
    options = []
    for left in range(8, depth, 8):
        for chunk in range(1, 65):
            if (depth - left) % chunk == 0:
                options.append((abs(left - TAIL) + 2 * abs(chunk - CHUNK), left, chunk))
    _, left, chunk = min(options)
    parts, at = [], 0
    for size in (16, 32, 48):
        if left - at > size:
            parts.append(size)
            at += size
    parts.append(left - at)
    parts.sort(reverse=True)
    return (depth - left) // chunk, chunk, left, [(sum(parts[:j]), size) for j, size in enumerate(parts)]


def work_plan(n_tm, spans, depth):
    big, chunk = spans[:2]
    helping = n_tm >= 4
    helped = n_tm - 3
    half = min(max(round(depth * SHARE / chunk), 1), big)
    pairs = []
    for owner in range(n_tm - 1):
        low = half if helping and owner == helped else 0
        pairs.append((owner, owner + 1, low, big, True, owner % 2 == 0))
    if helping:
        pairs.append((helped, 0, 0, half, False, True))
    return helping, helped, half, pairs


def meeting_plan(n_tm, n_lon, pairs, pieces, helping, helped):
    met = [set() for _ in range(n_tm)]

    def meet(a, b, shift):
        if a != b or shift % n_lon:
            met[a].add((b, shift % n_lon))
            met[b].add((a, -shift % n_lon))

    for owner, worker, _, _, _, direct in pairs:
        meet(owner, worker, 0)
        for piece in pieces:
            meet(owner if direct else worker, worker, -piece[0])
    if helping:
        meet(0, helped + 1, 0)
    return [sorted(entry) for entry in met]


def kernel(plan, spans, depth, sizes, state, counts, lists, *rest_refs):
    slots, pieces, n_src = plan
    big, chunk, left, parts = spans
    arrays, result, scratch = rest_refs[:5], rest_refs[5], rest_refs[6:]
    n_tm, n_lat, n_lon = sizes
    n_pieces = len(pieces)
    own, remotes, tail_remotes = scratch[0], scratch[1 : 1 + n_pieces], scratch[1 + n_pieces : 1 + 2 * n_pieces]
    (
        mine, prev, m_sem, r_sem, counts_s, lists_s, *arrays_v, flat, params, given, matrix, adv, f_end, ends, tail_mine,
        tail_own, adv_t, own_send, own_recv, x_send, f_send, x_recv, h_send, h_recv, t_send, t_recv, p_send, p_recv, a_sem,
    ) = scratch[1 + 2 * n_pieces :]
    rows, cols = state.shape[1:]
    tm, lat, lon = lax.axis_index("tm"), lax.axis_index("lat"), lax.axis_index("lon")
    helping, helped, half, pairs = work_plan(n_tm, spans, depth)
    n_parts = len(parts)
    order = list(range(EDGE)) + list(range(rows - EDGE, rows)) + list(range(EDGE, rows - EDGE))
    head = big * chunk

    is_helper = tm == 0
    first, last = jnp.int32(0), jnp.int32(0)
    for _, worker, low, high, _, _ in pairs:
        first = jnp.where(tm == worker, low, first)
        last = jnp.where(tm == worker, high, last)
    tailed = tm > 0

    aux = [
        pltpu.make_async_copy(source, place, a_sem.at[i])
        for i, (source, place) in enumerate(
            [(counts, counts_s), (lists, lists_s)]
            + [(array.at[0], place) for array, place in zip(arrays, arrays_v)]
        )
    ]
    to_mine = pltpu.make_async_copy(state, mine, m_sem)
    to_result = pltpu.make_async_copy(state, result, r_sem)
    owning = tm < n_tm - 1

    barrier = pltpu.get_barrier_semaphore()
    greeted = jnp.int32(0)

    def greet(condition, devices):
        @pl.when(condition)
        def _():
            for device in devices:
                pl.semaphore_signal(barrier, inc=1, device_id=device, device_id_type=MESH)

        return jnp.where(condition, len(devices), 0)

    for t, entry in enumerate(meeting_plan(n_tm, n_lon, pairs, pieces, helping, helped)):
        greeted += greet(
            tm == t, [{"tm": jnp.int32(b), "lon": lax.rem(lon + shift, n_lon)} for b, shift in entry]
        )
    greeted += greet(lat > 0, [{"lat": lat - 1}]) + greet(lat < n_lat - 1, [{"lat": lat + 1}])

    @pl.when(owning)
    def _():
        for copy in aux:
            copy.start()

    pl.semaphore_wait(barrier, greeted)

    def span(k):
        return k * chunk, chunk

    def own_copy(worker, k):
        part = pl.ds(*span(k))
        return pltpu.make_async_remote_copy(
            src_ref=state.at[part], dst_ref=own.at[part], send_sem=own_send.at[k], recv_sem=own_recv.at[k],
            device_id={"tm": jnp.int32(worker)}, device_id_type=MESH,
        )

    def x_copies(worker, k, direct):
        part = pl.ds(*span(k))
        source, sems = (state, x_send) if direct else (own, f_send)
        copies = []
        for i, (offset, block, number, _) in enumerate(pieces):
            copies.append(
                pltpu.make_async_remote_copy(
                    src_ref=source.at[part, :, pl.ds(block * BLK, number * BLK)],
                    dst_ref=remotes[i].at[part],
                    send_sem=sems.at[i, k], recv_sem=x_recv.at[i, k],
                    device_id={"tm": jnp.int32(worker), "lon": lax.rem(lon - offset + 2 * n_lon, n_lon)},
                    device_id_type=MESH,
                )
            )
        return copies

    def own_tail_copy(worker):
        return pltpu.make_async_remote_copy(
            src_ref=tail_mine, dst_ref=tail_own, send_sem=own_send.at[big], recv_sem=own_recv.at[big],
            device_id={"tm": jnp.int32(worker)}, device_id_type=MESH,
        )

    def x_tail_copies(worker, group, j, direct):
        at, size = parts[j]
        places = pl.ds(0, 2 * EDGE) if group == 0 else pl.ds(2 * EDGE, rows - 2 * EDGE)
        source, sems = (tail_mine, x_send) if direct else (tail_own, f_send)
        k = big + group * n_parts + j
        copies = []
        for i, (offset, block, number, _) in enumerate(pieces):
            copies.append(
                pltpu.make_async_remote_copy(
                    src_ref=source.at[places, pl.ds(at, size), pl.ds(block * BLK, number * BLK)],
                    dst_ref=tail_remotes[i].at[places, pl.ds(at, size)],
                    send_sem=sems.at[i, k], recv_sem=x_recv.at[i, k],
                    device_id={"tm": jnp.int32(worker), "lon": lax.rem(lon - offset + 2 * n_lon, n_lon)},
                    device_id_type=MESH,
                )
            )
        return copies

    def each_tail(act):
        for group in range(2):
            for j in range(n_parts):
                act(group, j)

    def prm_copy(worker, slot):
        return pltpu.make_async_remote_copy(
            src_ref=params, dst_ref=given, send_sem=p_send.at[slot], recv_sem=p_recv,
            device_id={"tm": jnp.int32(worker)}, device_id_type=MESH,
        )

    def halo_refs(k):
        if isinstance(k, int) and k < 0:
            at, size = parts[-1 - k]
            return lambda r: adv_t.at[pl.ds(r, 2), pl.ds(at, size)], big - 1 - k
        return lambda r: adv.at[k, pl.ds(r, 2)], k

    def halo_up(k):
        view, sem = halo_refs(k)
        return pltpu.make_async_remote_copy(
            src_ref=view(rows), dst_ref=view(0), send_sem=h_send.at[0, sem], recv_sem=h_recv.at[0, sem],
            device_id={"lat": lat + 1}, device_id_type=MESH,
        )

    def halo_down(k):
        view, sem = halo_refs(k)
        return pltpu.make_async_remote_copy(
            src_ref=view(2), dst_ref=view(rows + 2), send_sem=h_send.at[1, sem], recv_sem=h_recv.at[1, sem],
            device_id={"lat": lat - 1}, device_id_type=MESH,
        )

    def end_copy(k):
        return pltpu.make_async_remote_copy(
            src_ref=ends.at[k], dst_ref=prev.at[pl.ds(k * chunk, chunk)], send_sem=t_send.at[k], recv_sem=t_recv.at[k],
            device_id={"tm": jnp.int32(helped + 1)}, device_id_type=MESH,
        )

    def loop(low, high, act):
        lax.fori_loop(low, high, lambda c, _: (act(c), 0)[1], 0)

    def start_all(copies):
        for copy in copies:
            copy.start()

    for owner, worker, low, high, tail, direct in pairs:

        @pl.when(tm == owner)
        def _():
            if direct:
                early = min(low + 2, high)
                loop(low, low + 1, lambda k: start_all(x_copies(worker, k, True)))
                loop(low, early, lambda k: own_copy(worker, k).start())
                loop(low + 1, high, lambda k: start_all(x_copies(worker, k, True)))
                loop(early, high, lambda k: own_copy(worker, k).start())
            else:
                loop(low, high, lambda k: own_copy(worker, k).start())

    to_mine.start()
    pl.when(tm == 0)(to_result.start)

    @pl.when(lat == 0)
    def _():
        adv[:, 0:2] = jnp.zeros((big, 2, chunk, cols), adv.dtype)
        adv_t[0:2] = jnp.zeros((2, left, cols), adv.dtype)

    @pl.when(lat == n_lat - 1)
    def _():
        adv[:, rows + 2 : rows + 4] = jnp.zeros((big, 2, chunk, cols), adv.dtype)
        adv_t[rows + 2 : rows + 4] = jnp.zeros((2, left, cols), adv.dtype)

    def prepare():
        for copy in aux:
            copy.wait()
        entry, offset, lon_fraction, lat_shift, lat_fraction = [v[...] for v in arrays_v]
        per_list = lists.shape[1]
        for _ in range((per_list - 1) // 2):
            entry = jnp.where(entry >= counts_s[0, 0], entry - counts_s[0, 0], entry)
        blocks = cols // BLK
        total = blocks * n_lon
        for r in range(rows):
            for g in range(blocks):
                wanted = entry[r : r + 1, g * BLK : (g + 1) * BLK]
                chosen = jnp.zeros((1, BLK), jnp.int32)
                for k in range(per_list):
                    q = lists_s[0, k, g, r] - lon * blocks + blocks + blocks // 2 + total
                    q = lax.rem(q, total)
                    slot = jnp.int32(slots[0])
                    for i in range(1, len(slots)):
                        slot = jnp.where(q == i, slots[i], slot)
                    chosen = jnp.where(wanted == k, slot, chosen)
                params[1, r : r + 1, g * BLK : (g + 1) * BLK] = chosen.astype(jnp.float32)
        params[0] = offset.astype(jnp.float32)
        for node, weight in enumerate(cubic_weights(lon_fraction)):
            params[2 + node] = weight.astype(jnp.bfloat16).astype(jnp.float32)
        lat_weights = cubic_weights(lat_fraction)
        for shift in range(-2, 3):
            coefficient = jnp.zeros((rows, cols), jnp.float32)
            for node in range(4):
                coefficient = coefficient + jnp.where(
                    lat_shift + node - 1 == shift, lat_weights[node], 0.0
                )
            params[8 + shift] = coefficient

    def build(r):
        offset, slot = given[0, pl.ds(r, 1), :], given[1, pl.ds(r, 1), :]
        gap = lax.broadcasted_iota(jnp.int32, (BLK, cols), 0).astype(jnp.float32) - offset
        value = jnp.zeros((BLK, cols), jnp.float32)
        for node in range(4):
            weight = given[2 + node, pl.ds(r, 1), :]
            value = jnp.where(gap == node - 1.0, weight, value)
        for q in range(n_src):
            matrix[r, q * BLK : (q + 1) * BLK, :] = jnp.where(slot == q, value, 0.0).astype(
                jnp.bfloat16
            )

    def send_halos(k):
        @pl.when(lat < n_lat - 1)
        def _():
            halo_up(k).start()

        @pl.when(lat > 0)
        def _():
            halo_down(k).start()

    def spread(buffer, begin, size, at):
        for b in range(buffer.shape[2] // BLK):
            part = buffer[pl.ds(begin, size), :, b * BLK : (b + 1) * BLK].astype(jnp.float32)
            flat[at + b, 0 : size * rows] = part.reshape(size * rows, BLK)
        return at + buffer.shape[2] // BLK

    def advect(k):
        at = 0
        for buffer in (own, *remotes):
            at = spread(buffer, k * chunk, chunk, at)
        for place, r in enumerate(order):
            sources = [
                flat[q, pl.ds(r, chunk, stride=rows), :].astype(jnp.bfloat16)
                for q in range(n_src)
            ]
            total = jnp.dot(
                jnp.concatenate(sources, axis=1), matrix[r], preferred_element_type=jnp.float32
            )
            adv[k, r + 2] = total.astype(adv.dtype)
            if place == 2 * EDGE:
                send_halos(k)

    def lay_tail():
        for at, size in parts:
            spread(mine, head + at, size, 0)
            for place, r in enumerate(order):
                for b in range(cols // BLK):
                    tail_mine[place, at : at + size, b * BLK : (b + 1) * BLK] = flat[
                        b, pl.ds(r, size, stride=rows), :
                    ].astype(tail_mine.dtype)

    def advect_tail(group, j):
        at, size = parts[j]
        for place in range(0, 2 * EDGE) if group == 0 else range(2 * EDGE, rows):
            r = order[place]
            sources = [buffer[place, at : at + size] for buffer in (tail_own, *tail_remotes)]
            total = jnp.dot(
                jnp.concatenate(sources, axis=1), matrix[r], preferred_element_type=jnp.float32
            )
            adv_t[r + 2, at : at + size] = total.astype(adv.dtype)
        if group == 0:
            send_halos(-1 - j)

    def finish(k):
        if isinstance(k, int) and k < 0:
            at, size = parts[-1 - k]
            begin, field = head + at, lambda r: adv_t[r, at : at + size]
        else:
            begin, size, field = k * chunk, chunk, lambda r: adv[k, r]

        def interpolate(r):
            total = None
            for shift in range(5):
                term = given[6 + shift, r : r + 1, :] * field(r + shift).astype(jnp.float32)
                total = term if total is None else total + term
            for b in range(cols // BLK):
                f_end[b, pl.ds(r, size, stride=rows), :] = total[:, b * BLK : (b + 1) * BLK]

        for r in range(2, rows - 2):
            interpolate(r)

        @pl.when(lat > 0)
        def _():
            halo_up(k).wait_recv()

        @pl.when(lat < n_lat - 1)
        def _():
            halo_down(k).wait_recv()

        for r in (0, 1, rows - 2, rows - 1):
            interpolate(r)

        @pl.when(tailed)
        def _():
            for b in range(cols // BLK):
                part = f_end[b, 0 : size * rows].reshape(size, rows, BLK).astype(ends.dtype)
                place = (pl.ds(begin, size), slice(None), slice(b * BLK, (b + 1) * BLK))
                result[place] = (mine[place].astype(jnp.float32) - part.astype(jnp.float32)).astype(result.dtype)

        if helping and not (isinstance(k, int) and k < 0):

            @pl.when(is_helper)
            def _():
                for b in range(cols // BLK):
                    part = f_end[b, 0 : size * rows].reshape(size, rows, BLK).astype(ends.dtype)
                    ends[k, :, :, b * BLK : (b + 1) * BLK] = part
                end_copy(k).start()

    def collect(k):
        place = pl.ds(k * chunk, chunk)
        end_copy(k).wait_recv()
        moved = prev[place].astype(jnp.float32)
        result[place] = (mine[place].astype(jnp.float32) - moved).astype(result.dtype)

    pl.when(owning)(prepare)

    for slot, (owner, worker, *_) in enumerate(pairs):
        pl.when(tm == owner)(prm_copy(worker, slot).start)

    to_mine.wait()
    pl.when(owning)(lay_tail)
    for owner, worker, _, _, tail, direct in pairs:
        if tail:

            @pl.when(tm == owner)
            def _():
                own_tail_copy(worker).start()
                if direct:
                    each_tail(lambda group, j: start_all(x_tail_copies(worker, group, j, True)))

    for _, worker, low, high, tail, direct in pairs:
        if not direct:

            @pl.when(tm == worker)
            def _():
                def forward(k):
                    own_copy(0, k).wait_recv()
                    start_all(x_copies(worker, k, False))

                loop(low, high, forward)
                own_tail_copy(0).wait_recv()
                each_tail(lambda group, j: start_all(x_tail_copies(worker, group, j, False)))

    direct_own = jnp.bool_(True)
    for _, worker, _, _, _, direct in pairs:
        if not direct:
            direct_own = jnp.logical_and(direct_own, tm != worker)

    def land(k):
        @pl.when(direct_own)
        def _():
            own_copy(0, k).wait_recv()

        for copy in x_copies(0, k, True):
            copy.wait_recv()

    def land_tail(group, j):
        for copy in x_tail_copies(0, group, j, True):
            copy.wait_recv()

    collector = tm == helped + 1

    @pl.when(jnp.logical_or(tailed, first < last))
    def _():
        prm_copy(0, 0).wait_recv()
        loop(0, rows, build)

        def step(c):
            @pl.when(c < last)
            def _():
                land(c)
                advect(c)

            @pl.when(c > first)
            def _():
                finish(c - 1)

            if helping:

                @pl.when(jnp.logical_and(collector, c - first < half))
                def _():
                    collect(c - first)

        loop(first, last + 1, step)

    @pl.when(tailed)
    def _():
        @pl.when(direct_own)
        def _():
            own_tail_copy(0).wait_recv()

        for j in range(n_parts):
            land_tail(0, j)
            advect_tail(0, j)

    if helping:

        @pl.when(collector)
        def _():
            loop(jnp.minimum(last + 1 - first, half), half, collect)

    @pl.when(tailed)
    def _():
        for j in range(n_parts):
            land_tail(1, j)
            advect_tail(1, j)
            finish(-1 - j)

    pl.when(tm == 0)(to_result.wait)

    for slot, (owner, worker, low, high, tail, direct) in enumerate(pairs):

        @pl.when(tm == owner)
        def _():
            prm_copy(worker, slot).wait_send()

            def sent(k):
                own_copy(worker, k).wait_send()
                if direct:
                    for copy in x_copies(worker, k, True):
                        copy.wait_send()

            def sent_tail(group, j):
                for copy in x_tail_copies(worker, group, j, True):
                    copy.wait_send()

            loop(low, high, sent)
            if tail:
                own_tail_copy(worker).wait_send()
                if direct:
                    each_tail(sent_tail)

        @pl.when(tm == worker)
        def _():
            def settle_halos(k):
                @pl.when(lat < n_lat - 1)
                def _():
                    halo_up(k).wait_send()

                @pl.when(lat > 0)
                def _():
                    halo_down(k).wait_send()

            def settle(k):
                if not direct:
                    for copy in x_copies(worker, k, False):
                        copy.wait_send()
                settle_halos(k)
                if worker == 0:
                    end_copy(k).wait_send()

            def settle_tail(group, j):
                if not direct:
                    for copy in x_tail_copies(worker, group, j, False):
                        copy.wait_send()
                if group == 0:
                    settle_halos(-1 - j)

            loop(low, high, settle)
            if tail:
                each_tail(settle_tail)


def body(sizes, state, band_counts, dep_blocks, lon_entry, lon_offset, lon_frac, lat_offset, lat_frac):
    fields_n, levels, rows, cols = state.shape[1:]
    depth, blocks = fields_n * levels, cols // BLK
    n_tm, n_lat, n_lon = sizes
    plan = source_plan(blocks, n_lon)
    _, pieces, n_src = plan
    spans = span_plan(depth)
    big, chunk, left, parts = spans
    marks = big + 2 * len(parts)
    helping, _, half, pairs = work_plan(n_tm, spans, depth)
    flat = state.reshape(depth, rows, cols)

    lists = jnp.transpose(dep_blocks, (0, 3, 2, 1))
    dma = pltpu.SemaphoreType.DMA
    n_pieces = len(pieces)
    misfit = pl.pallas_call(
        functools.partial(kernel, plan, spans, depth, sizes),
        out_shape=pltpu.VMEM(flat.shape, flat.dtype),
        in_specs=[pl.BlockSpec(memory_space=pltpu.HBM)] * 8,
        out_specs=pl.BlockSpec(memory_space=pltpu.VMEM),
        scratch_shapes=[
            pltpu.VMEM(flat.shape, flat.dtype),
            *[pltpu.VMEM((depth, rows, p[2] * BLK), flat.dtype) for p in pieces],
            *[pltpu.VMEM((rows, left, p[2] * BLK), flat.dtype) for p in pieces],
            pltpu.VMEM(flat.shape, flat.dtype),
            pltpu.VMEM(flat.shape, flat.dtype),
            dma(()),
            dma(()),
            pltpu.SMEM(band_counts.shape, jnp.int32),
            pltpu.SMEM(lists.shape, jnp.int32),
            *[
                pltpu.VMEM((rows, cols), kind.dtype)
                for kind in (lon_entry, lon_offset, lon_frac, lat_offset, lat_frac)
            ],
            pltpu.VMEM((n_src, max(chunk, max(size for _, size in parts)) * rows, BLK), jnp.float32),
            pltpu.VMEM((11, rows, cols), jnp.float32),
            pltpu.VMEM((11, rows, cols), jnp.float32),
            pltpu.VMEM((rows, n_src * BLK, cols), jnp.bfloat16),
            pltpu.VMEM((big, rows + 4, chunk, cols), flat.dtype),
            pltpu.VMEM((blocks, max(chunk, max(size for _, size in parts)) * rows, BLK), jnp.float32),
            pltpu.VMEM((max(half, 1), chunk, rows, cols), flat.dtype),
            pltpu.VMEM((rows, left, cols), flat.dtype),
            pltpu.VMEM((rows, left, cols), flat.dtype),
            pltpu.VMEM((rows + 4, left, cols), flat.dtype),
            dma((marks,)),
            dma((marks,)),
            dma((n_pieces, marks)),
            dma((n_pieces, marks)),
            dma((n_pieces, marks)),
            dma((2, marks)),
            dma((2, marks)),
            dma((max(half, 1),)),
            dma((max(half, 1),)),
            dma((len(pairs),)),
            dma(()),
            dma((7,)),
        ],
        compiler_params=pltpu.CompilerParams(
            collective_id=0, has_side_effects=True, vmem_limit_bytes=60 * 1024 * 1024
        ),
    )(
        pltpu.with_memory_space_constraint(flat, pltpu.HBM),
        band_counts,
        *[
            pltpu.with_memory_space_constraint(array, pltpu.HBM)
            for array in (lists, lon_entry, lon_offset, lon_frac, lat_offset, lat_frac)
        ],
    )
    return misfit.reshape(state.shape)


def solution(mesh):
    placed = (
        P("tm", None, None, "lat", "lon"),
        P("tm", "lat"),
        P("tm", "lat", "lon", None),
        P("tm", "lat", "lon"),
        P("tm", "lat", "lon"),
        P("tm", "lat", "lon"),
        P("tm", "lat", "lon"),
        P("tm", "lat", "lon"),
    )
    sizes = tuple(mesh.shape[name] for name in ("tm", "lat", "lon"))
    return jax.shard_map(
        functools.partial(body, sizes),
        mesh=mesh,
        in_specs=placed,
        out_specs=P("tm", None, None, "lat", "lon"),
        check_vma=False,
    )
```

```python
import functools

import jax
import jax.numpy as jnp
from jax import lax
from jax.experimental import pallas as pl
from jax.experimental.pallas import tpu as pltpu
from jax.sharding import PartitionSpec as P

BLK = 128
CHUNK = 46
TAIL = 272
EDGE = 2
SHARE = 0.48
MESH = pl.DeviceIdType.MESH


def cubic_weights(fraction):
    return [
        -fraction * (fraction - 1.0) * (fraction - 2.0) / 6.0,
        (fraction + 1.0) * (fraction - 1.0) * (fraction - 2.0) / 2.0,
        -(fraction + 1.0) * fraction * (fraction - 2.0) / 2.0,
        (fraction + 1.0) * fraction * (fraction - 1.0) / 6.0,
    ]


def source_plan(blocks, devices):
    spread = blocks + blocks // 2
    count = min(3 * blocks, blocks * devices)
    slots, pieces, at = [None] * count, [], blocks
    for q in range(count):
        offset, block = divmod(q - spread, blocks)
        if offset % devices == 0:
            slots[q] = block
            continue
        if pieces and pieces[-1][0] == offset and pieces[-1][1] + pieces[-1][2] == block:
            pieces[-1][2] += 1
        else:
            pieces.append([offset, block, 1, at])
        slots[q] = at
        at += 1
    return slots, [tuple(piece) for piece in pieces], at


def span_plan(depth):
    options = []
    for left in range(8, depth, 8):
        for chunk in range(1, 65):
            if (depth - left) % chunk == 0:
                options.append((abs(left - TAIL) + 2 * abs(chunk - CHUNK), left, chunk))
    _, left, chunk = min(options)
    parts, at = [], 0
    while at < left:
        parts.append(min((16, 32, 48, 64)[min(len(parts), 3)], left - at))
        at += parts[-1]
    parts.sort(reverse=True)
    return (depth - left) // chunk, chunk, left, [(sum(parts[:j]), size) for j, size in enumerate(parts)]


def work_plan(n_tm, spans, depth):
    big, chunk = spans[:2]
    helping = n_tm >= 4
    helped = n_tm - 3
    half = min(max(round(depth * SHARE / chunk), 1), big)
    pairs = []
    for owner in range(n_tm - 1):
        low = half if helping and owner == helped else 0
        pairs.append((owner, owner + 1, low, big, True, owner % 2 == 0))
    if helping:
        pairs.append((helped, 0, 0, half, False, True))
    return helping, helped, half, pairs


def meeting_plan(n_tm, n_lon, pairs, pieces, helping, helped):
    met = [set() for _ in range(n_tm)]

    def meet(a, b, shift):
        if a != b or shift % n_lon:
            met[a].add((b, shift % n_lon))
            met[b].add((a, -shift % n_lon))

    for owner, worker, _, _, _, direct in pairs:
        meet(owner, worker, 0)
        for piece in pieces:
            meet(owner if direct else worker, worker, -piece[0])
    if helping:
        meet(0, helped + 1, 0)
    return [sorted(entry) for entry in met]


def kernel(plan, spans, depth, sizes, state, counts, lists, *rest_refs):
    slots, pieces, n_src = plan
    big, chunk, left, parts = spans
    arrays, result, scratch = rest_refs[:5], rest_refs[5], rest_refs[6:]
    n_tm, n_lat, n_lon = sizes
    n_pieces = len(pieces)
    own, remotes, tail_remotes = scratch[0], scratch[1 : 1 + n_pieces], scratch[1 + n_pieces : 1 + 2 * n_pieces]
    (
        mine, prev, m_sem, r_sem, counts_s, lists_s, *arrays_v, flat, params, given, matrix, adv, f_end, ends, tail_mine,
        tail_own, adv_t, own_send, own_recv, x_send, f_send, x_recv, h_send, h_recv, t_send, t_recv, p_send, p_recv, a_sem,
    ) = scratch[1 + 2 * n_pieces :]
    rows, cols = state.shape[1:]
    tm, lat, lon = lax.axis_index("tm"), lax.axis_index("lat"), lax.axis_index("lon")
    helping, helped, half, pairs = work_plan(n_tm, spans, depth)
    n_parts = len(parts)
    order = list(range(EDGE)) + list(range(rows - EDGE, rows)) + list(range(EDGE, rows - EDGE))
    head = big * chunk

    is_helper = tm == 0
    first, last = jnp.int32(0), jnp.int32(0)
    for _, worker, low, high, _, _ in pairs:
        first = jnp.where(tm == worker, low, first)
        last = jnp.where(tm == worker, high, last)
    tailed = tm > 0

    aux = [
        pltpu.make_async_copy(source, place, a_sem.at[i])
        for i, (source, place) in enumerate(
            [(counts, counts_s), (lists, lists_s)]
            + [(array.at[0], place) for array, place in zip(arrays, arrays_v)]
        )
    ]
    to_mine = pltpu.make_async_copy(state, mine, m_sem)
    to_result = pltpu.make_async_copy(state, result, r_sem)
    owning = tm < n_tm - 1

    barrier = pltpu.get_barrier_semaphore()
    greeted = jnp.int32(0)

    def greet(condition, devices):
        @pl.when(condition)
        def _():
            for device in devices:
                pl.semaphore_signal(barrier, inc=1, device_id=device, device_id_type=MESH)

        return jnp.where(condition, len(devices), 0)

    for t, entry in enumerate(meeting_plan(n_tm, n_lon, pairs, pieces, helping, helped)):
        greeted += greet(
            tm == t, [{"tm": jnp.int32(b), "lon": lax.rem(lon + shift, n_lon)} for b, shift in entry]
        )
    greeted += greet(lat > 0, [{"lat": lat - 1}]) + greet(lat < n_lat - 1, [{"lat": lat + 1}])

    @pl.when(owning)
    def _():
        for copy in aux:
            copy.start()

    pl.semaphore_wait(barrier, greeted)

    def span(k):
        return k * chunk, chunk

    def own_copy(worker, k):
        part = pl.ds(*span(k))
        return pltpu.make_async_remote_copy(
            src_ref=state.at[part], dst_ref=own.at[part], send_sem=own_send.at[k], recv_sem=own_recv.at[k],
            device_id={"tm": jnp.int32(worker)}, device_id_type=MESH,
        )

    def x_copies(worker, k, direct):
        part = pl.ds(*span(k))
        source, sems = (state, x_send) if direct else (own, f_send)
        copies = []
        for i, (offset, block, number, _) in enumerate(pieces):
            copies.append(
                pltpu.make_async_remote_copy(
                    src_ref=source.at[part, :, pl.ds(block * BLK, number * BLK)],
                    dst_ref=remotes[i].at[part],
                    send_sem=sems.at[i, k], recv_sem=x_recv.at[i, k],
                    device_id={"tm": jnp.int32(worker), "lon": lax.rem(lon - offset + 2 * n_lon, n_lon)},
                    device_id_type=MESH,
                )
            )
        return copies

    def own_tail_copy(worker):
        return pltpu.make_async_remote_copy(
            src_ref=tail_mine, dst_ref=tail_own, send_sem=own_send.at[big], recv_sem=own_recv.at[big],
            device_id={"tm": jnp.int32(worker)}, device_id_type=MESH,
        )

    def x_tail_copies(worker, group, j, direct):
        at, size = parts[j]
        places = pl.ds(0, 2 * EDGE) if group == 0 else pl.ds(2 * EDGE, rows - 2 * EDGE)
        source, sems = (tail_mine, x_send) if direct else (tail_own, f_send)
        k = big + group * n_parts + j
        copies = []
        for i, (offset, block, number, _) in enumerate(pieces):
            copies.append(
                pltpu.make_async_remote_copy(
                    src_ref=source.at[places, pl.ds(at, size), pl.ds(block * BLK, number * BLK)],
                    dst_ref=tail_remotes[i].at[places, pl.ds(at, size)],
                    send_sem=sems.at[i, k], recv_sem=x_recv.at[i, k],
                    device_id={"tm": jnp.int32(worker), "lon": lax.rem(lon - offset + 2 * n_lon, n_lon)},
                    device_id_type=MESH,
                )
            )
        return copies

    def each_tail(act):
        for group in range(2):
            for j in range(n_parts):
                act(group, j)

    def prm_copy(worker, slot):
        return pltpu.make_async_remote_copy(
            src_ref=params, dst_ref=given, send_sem=p_send.at[slot], recv_sem=p_recv,
            device_id={"tm": jnp.int32(worker)}, device_id_type=MESH,
        )

    def halo_refs(k):
        if isinstance(k, int) and k < 0:
            at, size = parts[-1 - k]
            return lambda r: adv_t.at[pl.ds(r, 2), pl.ds(at, size)], big - 1 - k
        return lambda r: adv.at[k, pl.ds(r, 2)], k

    def halo_up(k):
        view, sem = halo_refs(k)
        return pltpu.make_async_remote_copy(
            src_ref=view(rows), dst_ref=view(0), send_sem=h_send.at[0, sem], recv_sem=h_recv.at[0, sem],
            device_id={"lat": lat + 1}, device_id_type=MESH,
        )

    def halo_down(k):
        view, sem = halo_refs(k)
        return pltpu.make_async_remote_copy(
            src_ref=view(2), dst_ref=view(rows + 2), send_sem=h_send.at[1, sem], recv_sem=h_recv.at[1, sem],
            device_id={"lat": lat - 1}, device_id_type=MESH,
        )

    def end_copy(k):
        return pltpu.make_async_remote_copy(
            src_ref=ends.at[k], dst_ref=prev.at[pl.ds(k * chunk, chunk)], send_sem=t_send.at[k], recv_sem=t_recv.at[k],
            device_id={"tm": jnp.int32(helped + 1)}, device_id_type=MESH,
        )

    def loop(low, high, act):
        lax.fori_loop(low, high, lambda c, _: (act(c), 0)[1], 0)

    def start_all(copies):
        for copy in copies:
            copy.start()

    for owner, worker, low, high, tail, direct in pairs:

        @pl.when(tm == owner)
        def _():
            if direct:
                early = min(low + 2, high)
                loop(low, low + 1, lambda k: start_all(x_copies(worker, k, True)))
                loop(low, early, lambda k: own_copy(worker, k).start())
                loop(low + 1, high, lambda k: start_all(x_copies(worker, k, True)))
                loop(early, high, lambda k: own_copy(worker, k).start())
            else:
                loop(low, high, lambda k: own_copy(worker, k).start())

    to_mine.start()
    pl.when(tm == 0)(to_result.start)

    @pl.when(lat == 0)
    def _():
        adv[:, 0:2] = jnp.zeros((big, 2, chunk, cols), adv.dtype)
        adv_t[0:2] = jnp.zeros((2, left, cols), adv.dtype)

    @pl.when(lat == n_lat - 1)
    def _():
        adv[:, rows + 2 : rows + 4] = jnp.zeros((big, 2, chunk, cols), adv.dtype)
        adv_t[rows + 2 : rows + 4] = jnp.zeros((2, left, cols), adv.dtype)

    def prepare():
        for copy in aux:
            copy.wait()
        entry, offset, lon_fraction, lat_shift, lat_fraction = [v[...] for v in arrays_v]
        per_list = lists.shape[1]
        for _ in range((per_list - 1) // 2):
            entry = jnp.where(entry >= counts_s[0, 0], entry - counts_s[0, 0], entry)
        blocks = cols // BLK
        total = blocks * n_lon
        for r in range(rows):
            for g in range(blocks):
                wanted = entry[r : r + 1, g * BLK : (g + 1) * BLK]
                chosen = jnp.zeros((1, BLK), jnp.int32)
                for k in range(per_list):
                    q = lists_s[0, k, g, r] - lon * blocks + blocks + blocks // 2 + total
                    q = lax.rem(q, total)
                    slot = jnp.int32(slots[0])
                    for i in range(1, len(slots)):
                        slot = jnp.where(q == i, slots[i], slot)
                    chosen = jnp.where(wanted == k, slot, chosen)
                params[1, r : r + 1, g * BLK : (g + 1) * BLK] = chosen.astype(jnp.float32)
        params[0] = offset.astype(jnp.float32)
        for node, weight in enumerate(cubic_weights(lon_fraction)):
            params[2 + node] = weight.astype(jnp.bfloat16).astype(jnp.float32)
        lat_weights = cubic_weights(lat_fraction)
        for shift in range(-2, 3):
            coefficient = jnp.zeros((rows, cols), jnp.float32)
            for node in range(4):
                coefficient = coefficient + jnp.where(
                    lat_shift + node - 1 == shift, lat_weights[node], 0.0
                )
            params[8 + shift] = coefficient

    def build(r):
        offset, slot = given[0, pl.ds(r, 1), :], given[1, pl.ds(r, 1), :]
        gap = lax.broadcasted_iota(jnp.int32, (BLK, cols), 0).astype(jnp.float32) - offset
        value = jnp.zeros((BLK, cols), jnp.float32)
        for node in range(4):
            weight = given[2 + node, pl.ds(r, 1), :]
            value = jnp.where(gap == node - 1.0, weight, value)
        for q in range(n_src):
            matrix[r, q * BLK : (q + 1) * BLK, :] = jnp.where(slot == q, value, 0.0).astype(
                jnp.bfloat16
            )

    def send_halos(k):
        @pl.when(lat < n_lat - 1)
        def _():
            halo_up(k).start()

        @pl.when(lat > 0)
        def _():
            halo_down(k).start()

    def spread(buffer, begin, size, at):
        for b in range(buffer.shape[2] // BLK):
            part = buffer[pl.ds(begin, size), :, b * BLK : (b + 1) * BLK].astype(jnp.float32)
            flat[at + b, 0 : size * rows] = part.reshape(size * rows, BLK)
        return at + buffer.shape[2] // BLK

    def advect(k):
        at = 0
        for buffer in (own, *remotes):
            at = spread(buffer, k * chunk, chunk, at)
        for place, r in enumerate(order):
            sources = [
                flat[q, pl.ds(r, chunk, stride=rows), :].astype(jnp.bfloat16)
                for q in range(n_src)
            ]
            total = jnp.dot(
                jnp.concatenate(sources, axis=1), matrix[r], preferred_element_type=jnp.float32
            )
            adv[k, r + 2] = total.astype(adv.dtype)
            if place == 2 * EDGE:
                send_halos(k)

    def lay_tail():
        for at, size in parts:
            spread(mine, head + at, size, 0)
            for place, r in enumerate(order):
                for b in range(cols // BLK):
                    tail_mine[place, at : at + size, b * BLK : (b + 1) * BLK] = flat[
                        b, pl.ds(r, size, stride=rows), :
                    ].astype(tail_mine.dtype)

    def advect_tail(group, j):
        at, size = parts[j]
        for place in range(0, 2 * EDGE) if group == 0 else range(2 * EDGE, rows):
            r = order[place]
            sources = [buffer[place, at : at + size] for buffer in (tail_own, *tail_remotes)]
            total = jnp.dot(
                jnp.concatenate(sources, axis=1), matrix[r], preferred_element_type=jnp.float32
            )
            adv_t[r + 2, at : at + size] = total.astype(adv.dtype)
        if group == 0:
            send_halos(-1 - j)

    def finish(k):
        if isinstance(k, int) and k < 0:
            at, size = parts[-1 - k]
            begin, field = head + at, lambda r: adv_t[r, at : at + size]
        else:
            begin, size, field = k * chunk, chunk, lambda r: adv[k, r]

        def interpolate(r):
            total = None
            for shift in range(5):
                term = given[6 + shift, r : r + 1, :] * field(r + shift).astype(jnp.float32)
                total = term if total is None else total + term
            for b in range(cols // BLK):
                f_end[b, pl.ds(r, size, stride=rows), :] = total[:, b * BLK : (b + 1) * BLK]

        for r in range(2, rows - 2):
            interpolate(r)

        @pl.when(lat > 0)
        def _():
            halo_up(k).wait_recv()

        @pl.when(lat < n_lat - 1)
        def _():
            halo_down(k).wait_recv()

        for r in (0, 1, rows - 2, rows - 1):
            interpolate(r)

        @pl.when(tailed)
        def _():
            for b in range(cols // BLK):
                part = f_end[b, 0 : size * rows].reshape(size, rows, BLK).astype(ends.dtype)
                place = (pl.ds(begin, size), slice(None), slice(b * BLK, (b + 1) * BLK))
                result[place] = (mine[place].astype(jnp.float32) - part.astype(jnp.float32)).astype(result.dtype)

        if helping and not (isinstance(k, int) and k < 0):

            @pl.when(is_helper)
            def _():
                for b in range(cols // BLK):
                    part = f_end[b, 0 : size * rows].reshape(size, rows, BLK).astype(ends.dtype)
                    ends[k, :, :, b * BLK : (b + 1) * BLK] = part
                end_copy(k).start()

    def collect(k):
        place = pl.ds(k * chunk, chunk)
        end_copy(k).wait_recv()
        moved = prev[place].astype(jnp.float32)
        result[place] = (mine[place].astype(jnp.float32) - moved).astype(result.dtype)

    pl.when(owning)(prepare)

    for slot, (owner, worker, *_) in enumerate(pairs):
        pl.when(tm == owner)(prm_copy(worker, slot).start)

    to_mine.wait()
    pl.when(owning)(lay_tail)
    for owner, worker, _, _, tail, direct in pairs:
        if tail:

            @pl.when(tm == owner)
            def _():
                own_tail_copy(worker).start()
                if direct:
                    each_tail(lambda group, j: start_all(x_tail_copies(worker, group, j, True)))

    for _, worker, low, high, tail, direct in pairs:
        if not direct:

            @pl.when(tm == worker)
            def _():
                def forward(k):
                    own_copy(0, k).wait_recv()
                    start_all(x_copies(worker, k, False))

                loop(low, high, forward)
                own_tail_copy(0).wait_recv()
                each_tail(lambda group, j: start_all(x_tail_copies(worker, group, j, False)))

    direct_own = jnp.bool_(True)
    for _, worker, _, _, _, direct in pairs:
        if not direct:
            direct_own = jnp.logical_and(direct_own, tm != worker)

    def land(k):
        @pl.when(direct_own)
        def _():
            own_copy(0, k).wait_recv()

        for copy in x_copies(0, k, True):
            copy.wait_recv()

    def land_tail(group, j):
        for copy in x_tail_copies(0, group, j, True):
            copy.wait_recv()

    collector = tm == helped + 1

    @pl.when(jnp.logical_or(tailed, first < last))
    def _():
        prm_copy(0, 0).wait_recv()
        loop(0, rows, build)

        def step(c):
            @pl.when(c < last)
            def _():
                land(c)
                advect(c)

            @pl.when(c > first)
            def _():
                finish(c - 1)

            if helping:

                @pl.when(jnp.logical_and(collector, c - first < half))
                def _():
                    collect(c - first)

        loop(first, last + 1, step)

    @pl.when(tailed)
    def _():
        @pl.when(direct_own)
        def _():
            own_tail_copy(0).wait_recv()

        for j in range(n_parts):
            land_tail(0, j)
            advect_tail(0, j)

    if helping:

        @pl.when(collector)
        def _():
            loop(jnp.minimum(last + 1 - first, half), half, collect)

    @pl.when(tailed)
    def _():
        for j in range(n_parts):
            land_tail(1, j)
            advect_tail(1, j)
            finish(-1 - j)

    pl.when(tm == 0)(to_result.wait)

    for slot, (owner, worker, low, high, tail, direct) in enumerate(pairs):

        @pl.when(tm == owner)
        def _():
            prm_copy(worker, slot).wait_send()

            def sent(k):
                own_copy(worker, k).wait_send()
                if direct:
                    for copy in x_copies(worker, k, True):
                        copy.wait_send()

            def sent_tail(group, j):
                for copy in x_tail_copies(worker, group, j, True):
                    copy.wait_send()

            loop(low, high, sent)
            if tail:
                own_tail_copy(worker).wait_send()
                if direct:
                    each_tail(sent_tail)

        @pl.when(tm == worker)
        def _():
            def settle_halos(k):
                @pl.when(lat < n_lat - 1)
                def _():
                    halo_up(k).wait_send()

                @pl.when(lat > 0)
                def _():
                    halo_down(k).wait_send()

            def settle(k):
                if not direct:
                    for copy in x_copies(worker, k, False):
                        copy.wait_send()
                settle_halos(k)
                if worker == 0:
                    end_copy(k).wait_send()

            def settle_tail(group, j):
                if not direct:
                    for copy in x_tail_copies(worker, group, j, False):
                        copy.wait_send()
                if group == 0:
                    settle_halos(-1 - j)

            loop(low, high, settle)
            if tail:
                each_tail(settle_tail)


def body(sizes, state, band_counts, dep_blocks, lon_entry, lon_offset, lon_frac, lat_offset, lat_frac):
    fields_n, levels, rows, cols = state.shape[1:]
    depth, blocks = fields_n * levels, cols // BLK
    n_tm, n_lat, n_lon = sizes
    plan = source_plan(blocks, n_lon)
    _, pieces, n_src = plan
    spans = span_plan(depth)
    big, chunk, left, parts = spans
    marks = big + 2 * len(parts)
    helping, _, half, pairs = work_plan(n_tm, spans, depth)
    flat = state.reshape(depth, rows, cols)

    lists = jnp.transpose(dep_blocks, (0, 3, 2, 1))
    dma = pltpu.SemaphoreType.DMA
    n_pieces = len(pieces)
    misfit = pl.pallas_call(
        functools.partial(kernel, plan, spans, depth, sizes),
        out_shape=pltpu.VMEM(flat.shape, flat.dtype),
        in_specs=[pl.BlockSpec(memory_space=pltpu.HBM)] * 8,
        out_specs=pl.BlockSpec(memory_space=pltpu.VMEM),
        scratch_shapes=[
            pltpu.VMEM(flat.shape, flat.dtype),
            *[pltpu.VMEM((depth, rows, p[2] * BLK), flat.dtype) for p in pieces],
            *[pltpu.VMEM((rows, left, p[2] * BLK), flat.dtype) for p in pieces],
            pltpu.VMEM(flat.shape, flat.dtype),
            pltpu.VMEM(flat.shape, flat.dtype),
            dma(()),
            dma(()),
            pltpu.SMEM(band_counts.shape, jnp.int32),
            pltpu.SMEM(lists.shape, jnp.int32),
            *[
                pltpu.VMEM((rows, cols), kind.dtype)
                for kind in (lon_entry, lon_offset, lon_frac, lat_offset, lat_frac)
            ],
            pltpu.VMEM((n_src, max(chunk, max(size for _, size in parts)) * rows, BLK), jnp.float32),
            pltpu.VMEM((11, rows, cols), jnp.float32),
            pltpu.VMEM((11, rows, cols), jnp.float32),
            pltpu.VMEM((rows, n_src * BLK, cols), jnp.bfloat16),
            pltpu.VMEM((big, rows + 4, chunk, cols), flat.dtype),
            pltpu.VMEM((blocks, max(chunk, max(size for _, size in parts)) * rows, BLK), jnp.float32),
            pltpu.VMEM((max(half, 1), chunk, rows, cols), flat.dtype),
            pltpu.VMEM((rows, left, cols), flat.dtype),
            pltpu.VMEM((rows, left, cols), flat.dtype),
            pltpu.VMEM((rows + 4, left, cols), flat.dtype),
            dma((marks,)),
            dma((marks,)),
            dma((n_pieces, marks)),
            dma((n_pieces, marks)),
            dma((n_pieces, marks)),
            dma((2, marks)),
            dma((2, marks)),
            dma((max(half, 1),)),
            dma((max(half, 1),)),
            dma((len(pairs),)),
            dma(()),
            dma((7,)),
        ],
        compiler_params=pltpu.CompilerParams(
            collective_id=0, has_side_effects=True, vmem_limit_bytes=60 * 1024 * 1024
        ),
    )(
        pltpu.with_memory_space_constraint(flat, pltpu.HBM),
        band_counts,
        *[
            pltpu.with_memory_space_constraint(array, pltpu.HBM)
            for array in (lists, lon_entry, lon_offset, lon_frac, lat_offset, lat_frac)
        ],
    )
    return misfit.reshape(state.shape)


def solution(mesh):
    placed = (
        P("tm", None, None, "lat", "lon"),
        P("tm", "lat"),
        P("tm", "lat", "lon", None),
        P("tm", "lat", "lon"),
        P("tm", "lat", "lon"),
        P("tm", "lat", "lon"),
        P("tm", "lat", "lon"),
        P("tm", "lat", "lon"),
    )
    sizes = tuple(mesh.shape[name] for name in ("tm", "lat", "lon"))
    return jax.shard_map(
        functools.partial(body, sizes),
        mesh=mesh,
        in_specs=placed,
        out_specs=P("tm", None, None, "lat", "lon"),
        check_vma=False,
    )
```

```python
import functools

import jax
import jax.numpy as jnp
from jax import lax
from jax.experimental import pallas as pl
from jax.experimental.pallas import tpu as pltpu
from jax.sharding import PartitionSpec as P

BLK = 128
CHUNK = 69
TAIL = 272
EDGE = 2
SHARE = 0.48
EDGE_PARTS = (48, 96)
MIDDLE_PARTS = (32, 64)
MESH = pl.DeviceIdType.MESH


def cubic_weights(fraction):
    return [
        -fraction * (fraction - 1.0) * (fraction - 2.0) / 6.0,
        (fraction + 1.0) * (fraction - 1.0) * (fraction - 2.0) / 2.0,
        -(fraction + 1.0) * fraction * (fraction - 2.0) / 2.0,
        (fraction + 1.0) * fraction * (fraction - 1.0) / 6.0,
    ]


def source_plan(blocks, devices):
    spread = blocks + blocks // 2
    count = min(3 * blocks, blocks * devices)
    slots, pieces, at = [None] * count, [], blocks
    for q in range(count):
        offset, block = divmod(q - spread, blocks)
        if offset % devices == 0:
            slots[q] = block
            continue
        if pieces and pieces[-1][0] == offset and pieces[-1][1] + pieces[-1][2] == block:
            pieces[-1][2] += 1
        else:
            pieces.append([offset, block, 1, at])
        slots[q] = at
        at += 1
    return slots, [tuple(piece) for piece in pieces], at


def span_plan(depth):
    options = []
    for left in range(8, depth, 8):
        for chunk in range(1, 141):
            if (depth - left) % chunk == 0:
                options.append((abs(left - TAIL) + 2 * abs(chunk - CHUNK), left, chunk))
    _, left, chunk = min(options)
    parts = []
    for wanted in (EDGE_PARTS, MIDDLE_PARTS):
        sizes = []
        for size in wanted:
            if sum(sizes) + size < left:
                sizes.insert(0, size)
        sizes.insert(0, left - sum(sizes))
        parts.append([(sum(sizes[:j]), size) for j, size in enumerate(sizes)])
    return (depth - left) // chunk, chunk, left, parts


def work_plan(n_tm, spans, depth):
    big, chunk = spans[:2]
    helping = n_tm >= 4
    helped = n_tm - 3
    half = min(max(round(depth * SHARE / chunk), 1), big)
    pairs = []
    for owner in range(n_tm - 1):
        low = half if helping and owner == helped else 0
        pairs.append((owner, owner + 1, low, big, True, owner % 2 == 0))
    if helping:
        pairs.append((helped, 0, 0, half, False, True))
    return helping, helped, half, pairs


def meeting_plan(n_tm, n_lon, pairs, pieces, helping, helped):
    met = [set() for _ in range(n_tm)]

    def meet(a, b, shift):
        if a != b or shift % n_lon:
            met[a].add((b, shift % n_lon))
            met[b].add((a, -shift % n_lon))

    for owner, worker, _, _, _, direct in pairs:
        meet(owner, worker, 0)
        for piece in pieces:
            meet(owner if direct else worker, worker, -piece[0])
    if helping:
        meet(0, helped + 1, 0)
    return [sorted(entry) for entry in met]


def kernel(plan, spans, depth, sizes, state, counts, lists, *rest_refs):
    slots, pieces, n_src = plan
    big, chunk, left, parts = spans
    arrays, result, scratch = rest_refs[:5], rest_refs[5], rest_refs[6:]
    n_tm, n_lat, n_lon = sizes
    n_pieces = len(pieces)
    own, remotes, tail_remotes = scratch[0], scratch[1 : 1 + n_pieces], scratch[1 + n_pieces : 1 + 2 * n_pieces]
    (
        mine, prev, m_sem, r_sem, counts_s, lists_s, *arrays_v, flat, params, given, matrix, adv, f_end, ends, tail_mine,
        tail_own, adv_t, own_send, own_recv, x_send, f_send, x_recv, h_send, h_recv, t_send, t_recv, p_send, p_recv, a_sem,
    ) = scratch[1 + 2 * n_pieces :]
    rows, cols = state.shape[1:]
    tm, lat, lon = lax.axis_index("tm"), lax.axis_index("lat"), lax.axis_index("lon")
    helping, helped, half, pairs = work_plan(n_tm, spans, depth)
    order = list(range(EDGE)) + list(range(rows - EDGE, rows)) + list(range(EDGE, rows - EDGE))
    head = big * chunk

    is_helper = tm == 0
    first, last = jnp.int32(0), jnp.int32(0)
    for _, worker, low, high, _, _ in pairs:
        first = jnp.where(tm == worker, low, first)
        last = jnp.where(tm == worker, high, last)
    tailed = tm > 0

    aux = [
        pltpu.make_async_copy(source, place, a_sem.at[i])
        for i, (source, place) in enumerate(
            [(counts, counts_s), (lists, lists_s)]
            + [(array.at[0], place) for array, place in zip(arrays, arrays_v)]
        )
    ]
    to_mine = pltpu.make_async_copy(state, mine, m_sem)
    to_result = pltpu.make_async_copy(state, result, r_sem)
    owning = tm < n_tm - 1

    barrier = pltpu.get_barrier_semaphore()
    to_mine.start()
    greeted = jnp.int32(0)

    def greet(condition, devices):
        @pl.when(condition)
        def _():
            for device in devices:
                pl.semaphore_signal(barrier, inc=1, device_id=device, device_id_type=MESH)

        return jnp.where(condition, len(devices), 0)

    for t, entry in enumerate(meeting_plan(n_tm, n_lon, pairs, pieces, helping, helped)):
        greeted += greet(
            tm == t, [{"tm": jnp.int32(b), "lon": lax.rem(lon + shift, n_lon)} for b, shift in entry]
        )
    greeted += greet(lat > 0, [{"lat": lat - 1}]) + greet(lat < n_lat - 1, [{"lat": lat + 1}])

    @pl.when(owning)
    def _():
        for copy in aux:
            copy.start()

    pl.semaphore_wait(barrier, greeted)
    to_mine.wait()

    def span(k):
        return k * chunk, chunk

    def own_copy(worker, k):
        part = pl.ds(*span(k))
        return pltpu.make_async_remote_copy(
            src_ref=mine.at[part], dst_ref=own.at[part], send_sem=own_send.at[k], recv_sem=own_recv.at[k],
            device_id={"tm": jnp.int32(worker)}, device_id_type=MESH,
        )

    def x_copies(worker, k, direct):
        part = pl.ds(*span(k))
        source, sems = (mine, x_send) if direct else (own, f_send)
        copies = []
        for i, (offset, block, number, _) in enumerate(pieces):
            copies.append(
                pltpu.make_async_remote_copy(
                    src_ref=source.at[part, :, pl.ds(block * BLK, number * BLK)],
                    dst_ref=remotes[i].at[part],
                    send_sem=sems.at[i, k], recv_sem=x_recv.at[i, k],
                    device_id={"tm": jnp.int32(worker), "lon": lax.rem(lon - offset + 2 * n_lon, n_lon)},
                    device_id_type=MESH,
                )
            )
        return copies

    def own_tail_copy(worker):
        return pltpu.make_async_remote_copy(
            src_ref=tail_mine, dst_ref=tail_own, send_sem=own_send.at[big], recv_sem=own_recv.at[big],
            device_id={"tm": jnp.int32(worker)}, device_id_type=MESH,
        )

    def x_tail_copies(worker, group, j, direct):
        at, size = parts[group][j]
        places = pl.ds(0, 2 * EDGE) if group == 0 else pl.ds(2 * EDGE, rows - 2 * EDGE)
        source, sems = (tail_mine, x_send) if direct else (tail_own, f_send)
        k = big + group * len(parts[0]) + j
        copies = []
        for i, (offset, block, number, _) in enumerate(pieces):
            copies.append(
                pltpu.make_async_remote_copy(
                    src_ref=source.at[places, pl.ds(at, size), pl.ds(block * BLK, number * BLK)],
                    dst_ref=tail_remotes[i].at[places, pl.ds(at, size)],
                    send_sem=sems.at[i, k], recv_sem=x_recv.at[i, k],
                    device_id={"tm": jnp.int32(worker), "lon": lax.rem(lon - offset + 2 * n_lon, n_lon)},
                    device_id_type=MESH,
                )
            )
        return copies

    def each_tail(act):
        for group in range(2):
            for j in range(len(parts[group])):
                act(group, j)

    def prm_copy(worker, slot):
        return pltpu.make_async_remote_copy(
            src_ref=params, dst_ref=given, send_sem=p_send.at[slot], recv_sem=p_recv,
            device_id={"tm": jnp.int32(worker)}, device_id_type=MESH,
        )

    def halo_refs(k):
        if isinstance(k, int) and k < 0:
            at, size = parts[0][-1 - k]
            return lambda r: adv_t.at[pl.ds(r, 2), pl.ds(at, size)], big - 1 - k
        return lambda r: adv.at[k, pl.ds(r, 2)], k

    def halo_up(k):
        view, sem = halo_refs(k)
        return pltpu.make_async_remote_copy(
            src_ref=view(rows), dst_ref=view(0), send_sem=h_send.at[0, sem], recv_sem=h_recv.at[0, sem],
            device_id={"lat": lat + 1}, device_id_type=MESH,
        )

    def halo_down(k):
        view, sem = halo_refs(k)
        return pltpu.make_async_remote_copy(
            src_ref=view(2), dst_ref=view(rows + 2), send_sem=h_send.at[1, sem], recv_sem=h_recv.at[1, sem],
            device_id={"lat": lat - 1}, device_id_type=MESH,
        )

    def end_copy(k):
        return pltpu.make_async_remote_copy(
            src_ref=ends.at[k], dst_ref=prev.at[pl.ds(k * chunk, chunk)], send_sem=t_send.at[k], recv_sem=t_recv.at[k],
            device_id={"tm": jnp.int32(helped + 1)}, device_id_type=MESH,
        )

    def loop(low, high, act):
        lax.fori_loop(low, high, lambda c, _: (act(c), 0)[1], 0)

    def start_all(copies):
        for copy in copies:
            copy.start()

    for owner, worker, low, high, tail, direct in pairs:

        @pl.when(tm == owner)
        def _():
            if direct:
                early = min(low + 2, high)
                loop(low, low + 1, lambda k: start_all(x_copies(worker, k, True)))
                loop(low, early, lambda k: own_copy(worker, k).start())
                loop(low + 1, high, lambda k: start_all(x_copies(worker, k, True)))
                loop(early, high, lambda k: own_copy(worker, k).start())
            else:
                loop(low, high, lambda k: own_copy(worker, k).start())

    pl.when(tm == 0)(to_result.start)

    @pl.when(lat == 0)
    def _():
        adv[:, 0:2] = jnp.zeros((big, 2, chunk, cols), adv.dtype)
        adv_t[0:2] = jnp.zeros((2, left, cols), adv.dtype)

    @pl.when(lat == n_lat - 1)
    def _():
        adv[:, rows + 2 : rows + 4] = jnp.zeros((big, 2, chunk, cols), adv.dtype)
        adv_t[rows + 2 : rows + 4] = jnp.zeros((2, left, cols), adv.dtype)

    def prepare():
        for copy in aux:
            copy.wait()
        entry, offset, lon_fraction, lat_shift, lat_fraction = [v[...] for v in arrays_v]
        per_list = lists.shape[1]
        for _ in range((per_list - 1) // 2):
            entry = jnp.where(entry >= counts_s[0, 0], entry - counts_s[0, 0], entry)
        blocks = cols // BLK
        total = blocks * n_lon
        for r in range(rows):
            for g in range(blocks):
                wanted = entry[r : r + 1, g * BLK : (g + 1) * BLK]
                chosen = jnp.zeros((1, BLK), jnp.int32)
                for k in range(per_list):
                    q = lists_s[0, k, g, r] - lon * blocks + blocks + blocks // 2 + total
                    q = lax.rem(q, total)
                    slot = jnp.int32(slots[0])
                    for i in range(1, len(slots)):
                        slot = jnp.where(q == i, slots[i], slot)
                    chosen = jnp.where(wanted == k, slot, chosen)
                params[1, r : r + 1, g * BLK : (g + 1) * BLK] = chosen.astype(jnp.float32)
        params[0] = offset.astype(jnp.float32)
        for node, weight in enumerate(cubic_weights(lon_fraction)):
            params[2 + node] = weight.astype(jnp.bfloat16).astype(jnp.float32)
        lat_weights = cubic_weights(lat_fraction)
        for shift in range(-2, 3):
            coefficient = jnp.zeros((rows, cols), jnp.float32)
            for node in range(4):
                coefficient = coefficient + jnp.where(
                    lat_shift + node - 1 == shift, lat_weights[node], 0.0
                )
            params[8 + shift] = coefficient

    def build(r):
        offset, slot = given[0, pl.ds(r, 1), :], given[1, pl.ds(r, 1), :]
        gap = lax.broadcasted_iota(jnp.int32, (BLK, cols), 0).astype(jnp.float32) - offset
        value = jnp.zeros((BLK, cols), jnp.float32)
        for node in range(4):
            weight = given[2 + node, pl.ds(r, 1), :]
            value = jnp.where(gap == node - 1.0, weight, value)
        for q in range(n_src):
            matrix[r, q * BLK : (q + 1) * BLK, :] = jnp.where(slot == q, value, 0.0).astype(
                jnp.bfloat16
            )

    def send_halos(k):
        @pl.when(lat < n_lat - 1)
        def _():
            halo_up(k).start()

        @pl.when(lat > 0)
        def _():
            halo_down(k).start()

    def spread(buffer, begin, size, at):
        for b in range(buffer.shape[2] // BLK):
            part = buffer[pl.ds(begin, size), :, b * BLK : (b + 1) * BLK].astype(jnp.float32)
            flat[at + b, 0 : size * rows] = part.reshape(size * rows, BLK)
        return at + buffer.shape[2] // BLK

    def advect(k):
        at = 0
        for buffer in (own, *remotes):
            at = spread(buffer, k * chunk, chunk, at)
        for place, r in enumerate(order):
            sources = [
                flat[q, pl.ds(r, chunk, stride=rows), :].astype(jnp.bfloat16)
                for q in range(n_src)
            ]
            total = jnp.dot(
                jnp.concatenate(sources, axis=1), matrix[r], preferred_element_type=jnp.float32
            )
            adv[k, r + 2] = total.astype(adv.dtype)
            if place == 2 * EDGE:
                send_halos(k)

    def lay_tail():
        for at, size in parts[1]:
            spread(mine, head + at, size, 0)
            for place, r in enumerate(order):
                for b in range(cols // BLK):
                    tail_mine[place, at : at + size, b * BLK : (b + 1) * BLK] = flat[
                        b, pl.ds(r, size, stride=rows), :
                    ].astype(tail_mine.dtype)

    def advect_tail(group, j):
        at, size = parts[group][j]
        for place in range(0, 2 * EDGE) if group == 0 else range(2 * EDGE, rows):
            r = order[place]
            sources = [buffer[place, at : at + size] for buffer in (tail_own, *tail_remotes)]
            total = jnp.dot(
                jnp.concatenate(sources, axis=1), matrix[r], preferred_element_type=jnp.float32
            )
            adv_t[r + 2, at : at + size] = total.astype(adv.dtype)
        if group == 0:
            send_halos(-1 - j)

    def land_halos(k):
        @pl.when(lat > 0)
        def _():
            halo_up(k).wait_recv()

        @pl.when(lat < n_lat - 1)
        def _():
            halo_down(k).wait_recv()

    def finish(k):
        if isinstance(k, int) and k < 0:
            at, size = parts[1][-1 - k]
            begin, field = head + at, lambda r: adv_t[r, at : at + size]
        else:
            begin, size, field = k * chunk, chunk, lambda r: adv[k, r]

        def interpolate(r):
            total = None
            for shift in range(5):
                term = given[6 + shift, r : r + 1, :] * field(r + shift).astype(jnp.float32)
                total = term if total is None else total + term
            for b in range(cols // BLK):
                f_end[b, pl.ds(r, size, stride=rows), :] = total[:, b * BLK : (b + 1) * BLK]

        for r in range(2, rows - 2):
            interpolate(r)

        if not (isinstance(k, int) and k < 0):
            land_halos(k)
        for r in (0, 1, rows - 2, rows - 1):
            interpolate(r)

        @pl.when(tailed)
        def _():
            for b in range(cols // BLK):
                part = f_end[b, 0 : size * rows].reshape(size, rows, BLK).astype(ends.dtype)
                place = (pl.ds(begin, size), slice(None), slice(b * BLK, (b + 1) * BLK))
                result[place] = (mine[place].astype(jnp.float32) - part.astype(jnp.float32)).astype(result.dtype)

        if helping and not (isinstance(k, int) and k < 0):

            @pl.when(is_helper)
            def _():
                for b in range(cols // BLK):
                    part = f_end[b, 0 : size * rows].reshape(size, rows, BLK).astype(ends.dtype)
                    ends[k, :, :, b * BLK : (b + 1) * BLK] = part
                end_copy(k).start()

    def collect(k):
        place = pl.ds(k * chunk, chunk)
        end_copy(k).wait_recv()
        moved = prev[place].astype(jnp.float32)
        result[place] = (mine[place].astype(jnp.float32) - moved).astype(result.dtype)

    pl.when(owning)(prepare)

    for slot, (owner, worker, *_) in enumerate(pairs):
        pl.when(tm == owner)(prm_copy(worker, slot).start)

    pl.when(owning)(lay_tail)
    for owner, worker, _, _, tail, direct in pairs:
        if tail:

            @pl.when(tm == owner)
            def _():
                own_tail_copy(worker).start()
                if direct:
                    each_tail(lambda group, j: start_all(x_tail_copies(worker, group, j, True)))

    for _, worker, low, high, tail, direct in pairs:
        if not direct:

            @pl.when(tm == worker)
            def _():
                def forward(k):
                    own_copy(0, k).wait_recv()
                    start_all(x_copies(worker, k, False))

                loop(low, high, forward)
                own_tail_copy(0).wait_recv()
                each_tail(lambda group, j: start_all(x_tail_copies(worker, group, j, False)))

    direct_own = jnp.bool_(True)
    for _, worker, _, _, _, direct in pairs:
        if not direct:
            direct_own = jnp.logical_and(direct_own, tm != worker)

    def land(k):
        @pl.when(direct_own)
        def _():
            own_copy(0, k).wait_recv()

        for copy in x_copies(0, k, True):
            copy.wait_recv()

    def land_tail(group, j):
        for copy in x_tail_copies(0, group, j, True):
            copy.wait_recv()

    collector = tm == helped + 1

    @pl.when(jnp.logical_or(tailed, first < last))
    def _():
        prm_copy(0, 0).wait_recv()
        loop(0, rows, build)

        def step(c):
            @pl.when(c < last)
            def _():
                land(c)
                advect(c)

            @pl.when(c > first)
            def _():
                finish(c - 1)

            if helping:

                @pl.when(jnp.logical_and(collector, c - first < half))
                def _():
                    collect(c - first)

        loop(first, last + 1, step)

    @pl.when(tailed)
    def _():
        @pl.when(direct_own)
        def _():
            own_tail_copy(0).wait_recv()

        for j in range(len(parts[0])):
            land_tail(0, j)
            advect_tail(0, j)

    if helping:

        @pl.when(collector)
        def _():
            loop(jnp.minimum(last + 1 - first, half), half, collect)

    @pl.when(tailed)
    def _():
        for j in range(len(parts[1])):
            land_tail(1, j)
            advect_tail(1, j)
            if j == 0:
                for e in range(len(parts[0])):
                    land_halos(-1 - e)
            finish(-1 - j)

    pl.when(tm == 0)(to_result.wait)

    for slot, (owner, worker, low, high, tail, direct) in enumerate(pairs):

        @pl.when(tm == owner)
        def _():
            prm_copy(worker, slot).wait_send()

            def sent(k):
                own_copy(worker, k).wait_send()
                if direct:
                    for copy in x_copies(worker, k, True):
                        copy.wait_send()

            def sent_tail(group, j):
                for copy in x_tail_copies(worker, group, j, True):
                    copy.wait_send()

            loop(low, high, sent)
            if tail:
                own_tail_copy(worker).wait_send()
                if direct:
                    each_tail(sent_tail)

        @pl.when(tm == worker)
        def _():
            def settle_halos(k):
                @pl.when(lat < n_lat - 1)
                def _():
                    halo_up(k).wait_send()

                @pl.when(lat > 0)
                def _():
                    halo_down(k).wait_send()

            def settle(k):
                if not direct:
                    for copy in x_copies(worker, k, False):
                        copy.wait_send()
                settle_halos(k)
                if worker == 0:
                    end_copy(k).wait_send()

            def settle_tail(group, j):
                if not direct:
                    for copy in x_tail_copies(worker, group, j, False):
                        copy.wait_send()
                if group == 0:
                    settle_halos(-1 - j)

            loop(low, high, settle)
            if tail:
                each_tail(settle_tail)


def body(sizes, state, band_counts, dep_blocks, lon_entry, lon_offset, lon_frac, lat_offset, lat_frac):
    fields_n, levels, rows, cols = state.shape[1:]
    depth, blocks = fields_n * levels, cols // BLK
    n_tm, n_lat, n_lon = sizes
    plan = source_plan(blocks, n_lon)
    _, pieces, n_src = plan
    spans = span_plan(depth)
    big, chunk, left, parts = spans
    marks = big + len(parts[0]) + len(parts[1])
    widest = max(chunk, *[size for _, size in parts[1]])
    helping, _, half, pairs = work_plan(n_tm, spans, depth)
    flat = state.reshape(depth, rows, cols)

    lists = jnp.transpose(dep_blocks, (0, 3, 2, 1))
    dma = pltpu.SemaphoreType.DMA
    n_pieces = len(pieces)
    misfit = pl.pallas_call(
        functools.partial(kernel, plan, spans, depth, sizes),
        out_shape=pltpu.VMEM(flat.shape, flat.dtype),
        in_specs=[pl.BlockSpec(memory_space=pltpu.HBM)] * 8,
        out_specs=pl.BlockSpec(memory_space=pltpu.VMEM),
        scratch_shapes=[
            pltpu.VMEM(flat.shape, flat.dtype),
            *[pltpu.VMEM((depth, rows, p[2] * BLK), flat.dtype) for p in pieces],
            *[pltpu.VMEM((rows, left, p[2] * BLK), flat.dtype) for p in pieces],
            pltpu.VMEM(flat.shape, flat.dtype),
            pltpu.VMEM(flat.shape, flat.dtype),
            dma(()),
            dma(()),
            pltpu.SMEM(band_counts.shape, jnp.int32),
            pltpu.SMEM(lists.shape, jnp.int32),
            *[
                pltpu.VMEM((rows, cols), kind.dtype)
                for kind in (lon_entry, lon_offset, lon_frac, lat_offset, lat_frac)
            ],
            pltpu.VMEM((n_src, widest * rows, BLK), jnp.float32),
            pltpu.VMEM((11, rows, cols), jnp.float32),
            pltpu.VMEM((11, rows, cols), jnp.float32),
            pltpu.VMEM((rows, n_src * BLK, cols), jnp.bfloat16),
            pltpu.VMEM((big, rows + 4, chunk, cols), flat.dtype),
            pltpu.VMEM((blocks, widest * rows, BLK), jnp.float32),
            pltpu.VMEM((max(half, 1), chunk, rows, cols), flat.dtype),
            pltpu.VMEM((rows, left, cols), flat.dtype),
            pltpu.VMEM((rows, left, cols), flat.dtype),
            pltpu.VMEM((rows + 4, left, cols), flat.dtype),
            dma((marks,)),
            dma((marks,)),
            dma((n_pieces, marks)),
            dma((n_pieces, marks)),
            dma((n_pieces, marks)),
            dma((2, marks)),
            dma((2, marks)),
            dma((max(half, 1),)),
            dma((max(half, 1),)),
            dma((len(pairs),)),
            dma(()),
            dma((7,)),
        ],
        compiler_params=pltpu.CompilerParams(
            collective_id=0, has_side_effects=True, vmem_limit_bytes=60 * 1024 * 1024
        ),
    )(
        pltpu.with_memory_space_constraint(flat, pltpu.HBM),
        band_counts,
        *[
            pltpu.with_memory_space_constraint(array, pltpu.HBM)
            for array in (lists, lon_entry, lon_offset, lon_frac, lat_offset, lat_frac)
        ],
    )
    return misfit.reshape(state.shape)


def solution(mesh):
    placed = (
        P("tm", None, None, "lat", "lon"),
        P("tm", "lat"),
        P("tm", "lat", "lon", None),
        P("tm", "lat", "lon"),
        P("tm", "lat", "lon"),
        P("tm", "lat", "lon"),
        P("tm", "lat", "lon"),
        P("tm", "lat", "lon"),
    )
    sizes = tuple(mesh.shape[name] for name in ("tm", "lat", "lon"))
    return jax.shard_map(
        functools.partial(body, sizes),
        mesh=mesh,
        in_specs=placed,
        out_specs=P("tm", None, None, "lat", "lon"),
        check_vma=False,
    )
```
